512 devices in a mesh: grp: 8 (over y), exp: 64 (over x, z, core).
Axes of the slice: x: 4, y: 8, z: 8, core: 2. Of those that a mesh axis runs over, the one named last changes fastest.
Arguments:
- tokens: bfloat16 [65536, 1024], P(('grp', 'exp')), may hold values from -6 to 6
- w_in: bfloat16 [128, 1024, 768], P('exp', 'grp'), may hold values from -0.1875 to 0.1875
- w_out: bfloat16 [128, 384, 1024], P('exp', 'grp'), may hold values from -0.3125 to 0.3125
- moments_in: bfloat16 [128, 2, 1024, 768], P('exp', None, 'grp'), may hold values from -6 to 6
- moments_out: bfloat16 [128, 2, 384, 1024], P('exp', None, 'grp'), may hold values from -6 to 6
- expert_ids: int32 [65536, 8], P(('grp', 'exp')), may hold values from 0 to 95, all different within a row; in each aligned block of 128 rows (0 to 127, 128 to 255, ...) at most 16 rows name the same one
- route_weights: float32 [65536, 8], P(('grp', 'exp')), may hold values from 0.1 to 1
- old_plan: int32 [128], replicated, may hold values from 0 to 95, as said below
- new_plan: int32 [128], replicated, may hold values from 0 to 95, as said below
Outputs:
- mixed: bfloat16 [65536, 1024], P(('grp', 'exp'))
- new_w_in: bfloat16 [128, 1024, 768], P('exp', 'grp')
- new_w_out: bfloat16 [128, 384, 1024], P('exp', 'grp')
- new_moments_in: bfloat16 [128, 2, 1024, 768], P('exp', None, 'grp')
- new_moments_out: bfloat16 [128, 2, 384, 1024], P('exp', None, 'grp')
The draws below stay inside these ranges and needn't reach their ends.
Inputs may be any that keep to these rules, and one draw needn't show every extreme that they name: `expert_ids`: each row names 8 different experts. Among the rows of one device no expert is named more than 16 times, and in every draw some device names some expert exactly 16 times. `old_plan`: every expert is held by one or two slots; exactly 32 experts are held by two. `new_plan`: every expert is held by one or two slots; exactly 32 experts are held by two.
All inputs are finite; a program needn't handle non-finite values.
Results may differ from the reference program's by a relative error of at most 0.0057.
Values may be sent and summed in bfloat16 or wider, within the bound.
A program may use at most 64 MiB of HBM per device.

```python
import math
import jax
import jax.numpy as jnp
import numpy as np
from jax import lax

D = 1024
H = 384
TOP = 8
TOK_DEV = 128
EXPERTS = 96
SLOTS = 128
CAP = 16
TOKENS = 65536
N_GRP = 8
N_EXP = 64


def plan_draw(key, first, second):
    shuffled = jax.random.permutation(jax.random.fold_in(key, first), EXPERTS).astype(jnp.int32)
    doubled = jnp.concatenate([shuffled, shuffled[:SLOTS - EXPERTS]])
    placing = jax.random.permutation(jax.random.fold_in(key, second), SLOTS)
    return doubled[placing].astype(jnp.int32)


def draw_old_plan(key, part):
    return plan_draw(key, 11, 12)


def draw_new_plan(key, part):
    return plan_draw(key, 21, 22)


def level_of(rng, shape, cuts, low, high):
    factor_of = 1.0
    for axis_at, blocks in cuts:
        heights = jax.random.uniform(jax.random.fold_in(jax.random.fold_in(rng, 6), axis_at), (blocks,), jnp.float32, low / len(cuts), high / len(cuts))
        factor_of = factor_of * jnp.repeat(jnp.exp(heights), shape[axis_at] // blocks).reshape((-1,) + (1,) * (len(shape) - 1 - axis_at))
    return factor_of


def deal_out(rng, own, number, rows, amount, top, most, skew):
    ranking = jax.random.permutation(rng, amount)
    packed, common = shares(amount, rows * top, most, skew, True), shares(amount, rows * top, most, skew, False)
    places = jnp.arange(amount)

    def named(lengths, offset_by):
        used = int((lengths > 0).sum())
        fixed = max(1, used // 4)
        moved = fixed + (places - fixed + offset_by * (used - fixed)) % max(1, amount - fixed)
        return jnp.zeros((amount,), jnp.int32).at[ranking[jnp.where(places < fixed, places, moved)]].set(jnp.asarray(lengths, jnp.int32))

    lengths = jnp.where(number % 4 == 0, named(packed, number // 4), named(common, number - number // 4 - 1))
    mixed = jax.random.permutation(jax.random.fold_in(own, 3), amount)
    donor, taker = mixed[0:amount // 2 * 2:2], mixed[1:amount // 2 * 2:2]
    room = jnp.minimum(lengths[donor] - 1, most - lengths[taker]) // 2
    room = jnp.where((donor == ranking[0]) | (taker == ranking[0]) | (lengths[taker] == 0), 0, jnp.maximum(room, 0))
    moved = jax.random.randint(jax.random.fold_in(own, 4), (amount // 2,), 0, 1 << 20) % (room + 1)
    lengths = lengths.at[donor].add(-moved).at[taker].add(moved)
    labels = jnp.searchsorted(jnp.cumsum(lengths), jnp.arange(rows * top), side="right").astype(jnp.int32)
    listing = labels.reshape(top, rows).T
    listing = listing[jax.random.permutation(jax.random.fold_in(own, 1), rows)]
    offset_by = jax.random.randint(jax.random.fold_in(own, 2), (rows, 1), 0, top)
    return jnp.take_along_axis(listing, (jnp.arange(top)[None, :] + offset_by) % top, axis=1)


def shares(count, total, most, lean, full):
    weights = [(1 << 20) // math.isqrt(standing ** lean) + 1 for standing in range(1, count + 1)]
    largest = most if full else min(most, max(-(-total // count), total * weights[0] // sum(weights)))
    least = 1 if total - largest >= count - 1 else 0
    given, surplus = [largest] + [least] * (count - 1), total - largest - least * (count - 1)
    while surplus > 0:
        candidates = [i for i in range(1, count) if given[i] < largest] or [i for i in range(1, count) if given[i] < most]
        pool, left = sum([weights[i] for i in candidates]), surplus
        for i in candidates:
            extra = min(most - given[i], max(1, left * weights[i] // pool), surplus)
            given[i] = given[i] + extra
            surplus = surplus - extra
    return np.array(given)


def normal_values(rng, extent, spread, reach, pieces=(), kind=jnp.bfloat16):
    factor_of = level_of(rng, extent, pieces, -0.22, 0.18) if pieces else 1.0
    array = jax.random.normal(rng, extent, jnp.float32) * spread * factor_of
    return jnp.minimum(jnp.maximum(array, -reach), reach).astype(kind)


def setup_inputs(seed: int = 0) -> dict:
    seeds = jax.random.split(jax.random.key(seed), 10)
    tokens = normal_values(seeds[0], (TOKENS, D), 1.0, 6.0, ((0, 512),))
    w_in = normal_values(seeds[1], (SLOTS, D, 2 * H), D ** -0.5, 0.1875, ((0, 64), (1, 8)))
    w_out = normal_values(seeds[2], (SLOTS, H, D), H ** -0.5, 0.3125, ((0, 64), (1, 8)))
    moments_in = normal_values(seeds[3], (SLOTS, 2, D, 2 * H), 1.0, 6.0, ((0, 64), (2, 8)))
    moments_out = normal_values(seeds[4], (SLOTS, 2, H, D), 1.0, 6.0, ((0, 64), (2, 8)))
    expert_ids_keys = jax.random.split(jax.random.fold_in(seeds[5], 1), TOKENS // TOK_DEV)
    expert_ids_turns = jax.random.permutation(jax.random.fold_in(seeds[5], 3), TOKENS // TOK_DEV)
    expert_ids = jax.vmap(lambda own, number: deal_out(jax.random.fold_in(seeds[5], 2), own, number, TOK_DEV, EXPERTS, TOP, CAP, 2))(expert_ids_keys, expert_ids_turns).reshape((TOKENS, TOP))
    route_weights = jnp.clip(jnp.exp(math.log(1.0) - 2.3025851 * jax.random.uniform(seeds[6], (TOKENS, TOP), jnp.float32) ** level_of(seeds[6], (TOKENS, TOP), ((0, 512),), -0.2, 0.2)), 0.1, 1.0)
    old_plan = draw_old_plan(jax.random.fold_in(seeds[9], 71), 0)
    new_plan = draw_new_plan(jax.random.fold_in(seeds[9], 71), 0)
    return dict(tokens=tokens, w_in=w_in, w_out=w_out, moments_in=moments_in, moments_out=moments_out, expert_ids=expert_ids, route_weights=route_weights, old_plan=old_plan, new_plan=new_plan)


def reference(tokens, w_in, w_out, moments_in, moments_out, expert_ids, route_weights, old_plan, new_plan):
    slot_count = old_plan.shape[0]
    slot_index = jnp.arange(slot_count, dtype=jnp.int32)
    same_expert = new_plan[:, None] == old_plan[None, :]
    source = jnp.min(jnp.where(same_expert, slot_index[None, :], slot_count), axis=1).astype(jnp.int32)
    new_w_in = w_in[source]
    new_w_out = w_out[source]
    new_moments_in = moments_in[source]
    new_moments_out = moments_out[source]
    expert_index = jnp.arange(EXPERTS, dtype=jnp.int32)
    holders = new_plan[None, :] == expert_index[:, None]
    first_slot = jnp.min(jnp.where(holders, slot_index[None, :], slot_count), axis=1).astype(jnp.int32)
    expert_in = new_w_in[first_slot]
    expert_outw = new_w_out[first_slot]
    pair_expert = expert_ids.reshape(-1)
    order = jnp.argsort(pair_expert, stable=True).astype(jnp.int32)
    counts = jax.ops.segment_sum(jnp.ones_like(pair_expert), pair_expert, EXPERTS).astype(jnp.int32)
    starts = (jnp.cumsum(counts) - counts).astype(jnp.int32)
    most = N_GRP * N_EXP * CAP
    padded = jnp.concatenate([order, jnp.zeros((most,), jnp.int32)])
    share = route_weights / jnp.sum(route_weights, axis=1, keepdims=True)
    share_flat = share.reshape(-1)
    line = jnp.arange(most, dtype=jnp.int32)

    def one_expert(total, index):
        members = lax.dynamic_slice(padded, (starts[index],), (most,))
        valid = line < counts[index]
        token_index = members // TOP
        rows = tokens[token_index]
        both = jnp.dot(rows, expert_in[index], preferred_element_type=jnp.float32)
        hidden = (jax.nn.silu(both[:, :H]) * both[:, H:]).astype(jnp.bfloat16)
        result = jnp.dot(hidden, expert_outw[index], preferred_element_type=jnp.float32).astype(jnp.bfloat16)
        weight = jnp.where(valid, share_flat[members], jnp.zeros((), share_flat.dtype))
        total = total.at[token_index].add(weight[:, None] * result.astype(jnp.float32))
        return total, None

    total, _ = lax.scan(one_expert, jnp.zeros((tokens.shape[0], D), jnp.float32), expert_index)
    return (total.astype(jnp.bfloat16), new_w_in, new_w_out, new_moments_in, new_moments_out)
```

```python
import functools
import heapq

import jax
import jax.numpy as jnp
from jax import lax
from jax.experimental import pallas as pl
from jax.experimental.pallas import tpu as pltpu
from jax.sharding import PartitionSpec as P

TOP = 8
TOK = 128
D = 1024
H = 384
NX, NZ, NY = 4, 8, 8
META = 8
ROWS = TOK + META
CAP = 16
CHIPS = NX * NZ
MESH = pl.DeviceIdType.MESH
VMEM_LIMIT = 62 * 1024 * 1024
TILES = 432
CHUNK = 7


def order_of(items):
    free, heap, started, arrived, ops = {}, [], set(), set(), []

    def start_ready(now):
        for name, (link, size, deps) in items.items():
            if name not in started and all(d in arrived for d in deps):
                begin = max(now, free.get(link, 0.0))
                free[link] = begin + size
                heapq.heappush(heap, (free[link] + (600.0 if link[0] != "c" else 100.0), len(started), name))
                started.add(name)
                ops.append(("start", name))

    start_ready(0.0)
    while heap:
        now, _, name = heapq.heappop(heap)
        arrived.add(name)
        ops.append(("wait", name))
        start_ready(now)
    return ops


def split(lo, hi, s):
    mid = lo + ((hi - lo) // 2 + 7) // 8 * 8
    return (lo, mid) if s > 0 else (mid, hi)


def place():
    y = lax.axis_index("grp")
    e = lax.axis_index("exp")
    c = lax.rem(e, 2)
    r = e // 2
    return y, e, c, r // NZ, lax.rem(r, NZ)


def chip_at(x, z, dx, dz):
    return lax.rem(x + dx + NX, NX) * NZ + lax.rem(z + dz + NZ, NZ)


def neighbour(link):
    y, e, c, x, z = place()
    axis, s = link
    if axis == "x":
        return (y, 2 * chip_at(x, z, s, 0) + c)
    if axis == "z":
        return (y, 2 * chip_at(x, z, 0, s) + c)
    if axis == "y":
        return (lax.rem(y + s + NY, NY), e)
    return (y, e + 1 - 2 * c)


def greet(links):
    barrier = pltpu.get_barrier_semaphore()
    for link in links:
        pl.semaphore_signal(barrier, inc=1, device_id=neighbour(link), device_id_type=MESH)
    pl.semaphore_wait(barrier, len(links))


TORUS = (("x", 1), ("x", -1), ("z", 1), ("z", -1))


def gather_items(pr):
    row, items = D * 2 / 46.5, {}

    def rows_of(name):
        lo, hi = (0, pr) if name[0][0] == "P" else (pr, ROWS)
        half = name[-1] == (4 if name[0][1] == "Z" else 2)
        return split(lo, hi, name[-2]) if half else (lo, hi)

    def add(name, link, deps):
        lo, hi = rows_of(name)
        items[name] = (link, (hi - lo) * row, deps)

    for s in (1, -1):
        for d in (1, 2, 3, 4):
            add(("PZ", s, d), ("z", s), [("PZ", s, d - 1)] if d > 1 else [])
        for d in (1, 2):
            add(("QX", s, d), ("x", s), [("QX", s, d - 1)] if d > 1 else [])
    for s in (1, -1):
        for d in (1, 2, 3, 4):
            dep = lambda k: [(k, s, d - 1)] if d > 1 else []
            part = 0.5 if d == 4 else 1.0
            items[("WI", s, d)] = (("y", s), part * 2 * 128 * 768 * 2 / 46.5, dep("WI"))
            items[("WO", s, d)] = (("y", s), part * 2 * 48 * 1024 * 2 / 46.5, dep("WO"))
    for dz in (0, 1, 7, 2, 6, 3, 5, 4):
        for s in (1, -1):
            for d in (1, 2):
                if d == 2:
                    deps = [("PX", dz, s, 1)]
                elif dz == 0:
                    deps = []
                elif dz == 4:
                    deps = [("PZ", 1, 4), ("PZ", -1, 4)]
                else:
                    deps = [("PZ", -1, dz)] if dz < 4 else [("PZ", 1, 8 - dz)]
                add(("PX", dz, s, d), ("x", s), deps)
    for dx in (0, 1, 3, 2):
        for s in (1, -1):
            for d in (1, 2, 3, 4):
                if d > 1:
                    deps = [("QZ", dx, s, d - 1)]
                elif dx == 0:
                    deps = []
                elif dx == 2:
                    deps = [("QX", 1, 2), ("QX", -1, 2)]
                else:
                    deps = [("QX", -1, 1)] if dx == 1 else [("QX", 1, 1)]
                add(("QZ", dx, s, d), ("z", s), deps)
    for dy in range(NY):
        for k, size in (("WI", 393216), ("WO", 196608)):
            if dy == 0:
                deps = []
            elif dy == 4:
                deps = [(k, 1, 4), (k, -1, 4)]
            else:
                deps = [(k, -1, dy)] if dy < 4 else [(k, 1, 8 - dy)]
            items[("S" + k, dy)] = (("c", 0), size / 300.0, deps)
    return items, rows_of


def gather_kernel(pr, xt, wi, wo, g, gi, go, ssem, rsem, lsem):
    y, e, c, x, z = place()
    items, rows_of = gather_items(pr)
    index = {name: i for i, name in enumerate(items)}
    greet(TORUS + (("y", 1), ("y", -1), ("c", 0)))
    own = chip_at(x, z, 0, 0)
    span_i, span_o = wi.shape[1], wo.shape[1]

    def weights(k, dy, slots, core):
        ref, span = (gi, span_i) if k == "WI" else (go, span_o)
        at = pl.multiple_of(lax.rem(y + dy + NY, NY) * span, span)
        return ref.at[pl.ds(2 * core + slots[0], slots[1]), pl.ds(at, span)]

    def ends(name, shift):
        kind = name[0]
        if kind[0] == "S":
            k, dy = kind[1:], name[1]
            core = c if shift else 1 - c
            dst = weights(k, dy, (0, 2), core)
            return ((wi if k == "WI" else wo) if dy == 0 else dst), dst
        if kind[0] == "W":
            s, d = name[1:]
            slots = (0, 2) if d < 4 else ((0, 1) if s > 0 else (1, 1))
            dst = weights(kind, -s * (d - shift), slots, c)
            return ((wi if kind == "WI" else wo) if d == 1 else dst), dst
        lo, hi = rows_of(name)
        s, d = name[-2:]
        off = -s * (d - shift)
        if kind == "PZ":
            dx, dz = 0, off
        elif kind == "QX":
            dx, dz = off, 0
        elif kind == "PX":
            dx, dz = off, name[1]
        else:
            dx, dz = name[1], off
        dst = g.at[chip_at(x, z, dx, dz), pl.ds(lo, hi - lo)]
        mine = shift == 1 and dx % NX == 0 and dz % NZ == 0
        return (xt.at[pl.ds(lo, hi - lo)] if mine else dst), dst

    def copy(name, shift):
        src, dst = ends(name, shift)
        i = index[name]
        return pltpu.make_async_remote_copy(
            src_ref=src if shift else dst,
            dst_ref=dst,
            send_sem=ssem.at[i],
            recv_sem=rsem.at[i],
            device_id=neighbour(items[name][0]),
            device_id_type=MESH,
        )

    local = [
        pltpu.make_async_copy(xt, g.at[own], lsem.at[0]),
        pltpu.make_async_copy(wi, weights("WI", 0, (0, 2), c), lsem.at[1]),
        pltpu.make_async_copy(wo, weights("WO", 0, (0, 2), c), lsem.at[2]),
    ]
    for name_op in order_of(items):
        op, name = name_op
        if op == "start":
            copy(name, 1).start()
        else:
            copy(name, 0).wait_recv()
        if local and op == "wait":
            for item in local:
                item.start()
            done, local = local, []
    for item in done:
        item.wait()
    for name in items:
        copy(name, 1).wait_send()


def gather(pr, xt, wi, wo):
    count = len(gather_items(pr)[0])
    any_space = pl.BlockSpec(memory_space=pl.ANY)
    vmem = pl.BlockSpec(memory_space=pltpu.VMEM)
    return pl.pallas_call(
        functools.partial(gather_kernel, pr),
        out_shape=(
            jax.ShapeDtypeStruct((CHIPS, ROWS, D), jnp.bfloat16),
            jax.ShapeDtypeStruct((4, D, 2 * H), jnp.bfloat16),
            jax.ShapeDtypeStruct((4, H, D), jnp.bfloat16),
        ),
        in_specs=[vmem] * 3,
        out_specs=(any_space,) * 3,
        scratch_shapes=[
            pltpu.SemaphoreType.DMA((count,)),
            pltpu.SemaphoreType.DMA((count,)),
            pltpu.SemaphoreType.DMA((3,)),
        ],
        compiler_params=pltpu.CompilerParams(
            collective_id=0, has_side_effects=True, vmem_limit_bytes=VMEM_LIMIT
        ),
        cost_estimate=pl.CostEstimate(flops=0, bytes_accessed=200_000_000, transcendentals=0),
        name="gather",
    )(xt, wi, wo)


STEP = 8


def expert_kernel(es, g, wi, wo, part, gv, wiv, wov, xs, ys, cnt, wgt, rank, sel, outv, isem, wsem, osem):
    nchunk = CHIPS // STEP
    for n in range(nchunk):
        pltpu.make_async_copy(g.at[pl.ds(n * STEP, STEP)], gv.at[pl.ds(n * STEP, STEP)], isem.at[n]).start()
    for j in range(4):
        pltpu.make_async_copy(wi.at[j], wiv.at[j], wsem.at[j]).start()
        pltpu.make_async_copy(wo.at[j], wov.at[j], wsem.at[4 + j]).start()
    tri = (
        lax.broadcasted_iota(jnp.int32, (TOK, TOK), 0) <= lax.broadcasted_iota(jnp.int32, (TOK, TOK), 1)
    ).astype(jnp.bfloat16)
    line = lax.broadcasted_iota(jnp.int32, (CAP, TOK), 0).astype(jnp.float32)
    experts = [es[j].astype(jnp.float32) for j in range(4)]
    for n in range(nchunk):
        pltpu.make_async_copy(
            g.at[pl.ds(n * STEP, STEP)], gv.at[pl.ds(n * STEP, STEP)], isem.at[n]
        ).wait()

        def count(i, _):
            b = n * STEP + i
            meta = gv[b, TOK:ROWS, 0:256].astype(jnp.float32)
            ids, share = meta[:, 0:TOK], meta[:, TOK:256]
            named = [ids == experts[j] for j in range(4)]
            ones = [jnp.sum(jnp.where(m, 1.0, 0.0), axis=0, keepdims=True) for m in named]
            held = [jnp.sum(jnp.where(m, share, 0.0), axis=0, keepdims=True) for m in named]
            rows = pl.ds(pl.multiple_of(b * 8, 8), 8)
            cnt[rows, :] = jnp.concatenate(ones + ones, axis=0)
            wgt[rows, :] = jnp.concatenate(held + held, axis=0)
            return 0

        lax.fori_loop(0, STEP, count, 0)
        rows = pl.ds(n * STEP * 8, STEP * 8)
        chosen = cnt[rows, :]
        upto = jnp.dot(chosen.astype(jnp.bfloat16), tri, preferred_element_type=jnp.float32)
        rank[rows, :] = jnp.where(chosen > 0.5, upto - 1.0, -1.0)

        def pick(i, _):
            b = n * STEP + i
            rows = pl.ds(pl.multiple_of(b * 8, 8), 8)
            place8, held8 = rank[rows, :], wgt[rows, :]
            hit = [line == place8[j : j + 1, :] for j in range(4)]
            onehot = jnp.concatenate([jnp.where(m, 1.0, 0.0) for m in hit], axis=0)
            weight = jnp.concatenate(
                [jnp.where(hit[j], held8[j : j + 1, :], 0.0) for j in range(4)], axis=0
            )
            sel[b] = weight.astype(jnp.bfloat16)
            got = jnp.dot(
                onehot.astype(jnp.bfloat16), gv[b, 0:TOK, :], preferred_element_type=jnp.float32
            ).astype(jnp.bfloat16)
            at = pl.ds(pl.multiple_of(b * CAP, CAP), CAP)
            for j in range(4):
                xs[j, at, :] = got[j * CAP : (j + 1) * CAP, :]
            return 0

        lax.fori_loop(0, STEP, pick, 0, unroll=2)
    for j in range(4):
        pltpu.make_async_copy(wi.at[j], wiv.at[j], wsem.at[j]).wait()
        pltpu.make_async_copy(wo.at[j], wov.at[j], wsem.at[4 + j]).wait()

    def mlp(i, _):
        j, at = i // 2, pl.ds(pl.multiple_of(lax.rem(i, 2) * 256, 256), 256)
        both = jnp.dot(xs[j, at, :], wiv[j], preferred_element_type=jnp.float32)
        hidden = (jax.nn.silu(both[:, :H]) * both[:, H:]).astype(jnp.bfloat16)
        ys[j, at, :] = jnp.dot(hidden, wov[j], preferred_element_type=jnp.float32).astype(jnp.bfloat16)
        return 0

    lax.fori_loop(0, 8, mlp, 0)
    for n in range(nchunk):

        def spread(i, _):
            b = n * STEP + i
            at = pl.ds(pl.multiple_of(b * CAP, CAP), CAP)
            rows = jnp.concatenate([ys[j, at, :] for j in range(4)], axis=0)
            outv[b] = lax.dot_general(
                sel[b], rows, (((0,), (0,)), ((), ())), preferred_element_type=jnp.float32
            ).astype(jnp.bfloat16)
            return 0

        lax.fori_loop(0, STEP, spread, 0, unroll=2)
        pltpu.make_async_copy(outv.at[pl.ds(n * STEP, STEP)], part.at[pl.ds(n * STEP, STEP)], osem.at[n]).start()
    for n in range(nchunk):
        pltpu.make_async_copy(
            outv.at[pl.ds(n * STEP, STEP)], part.at[pl.ds(n * STEP, STEP)], osem.at[n]
        ).wait()


def experts_of(es, g, wi, wo):
    any_space = pl.BlockSpec(memory_space=pl.ANY)
    nchunk = CHIPS // STEP
    return pl.pallas_call(
        expert_kernel,
        out_shape=jax.ShapeDtypeStruct((CHIPS, TOK, D), jnp.bfloat16),
        in_specs=[pl.BlockSpec(memory_space=pltpu.SMEM)] + [any_space] * 3,
        out_specs=any_space,
        scratch_shapes=[
            pltpu.VMEM((CHIPS, ROWS, D), jnp.bfloat16),
            pltpu.VMEM((4, D, 2 * H), jnp.bfloat16),
            pltpu.VMEM((4, H, D), jnp.bfloat16),
            pltpu.VMEM((4, CHIPS * CAP, D), jnp.bfloat16),
            pltpu.VMEM((4, CHIPS * CAP, D), jnp.bfloat16),
            pltpu.VMEM((CHIPS * 8, TOK), jnp.float32),
            pltpu.VMEM((CHIPS * 8, TOK), jnp.float32),
            pltpu.VMEM((CHIPS * 8, TOK), jnp.float32),
            pltpu.VMEM((CHIPS, 4 * CAP, TOK), jnp.bfloat16),
            pltpu.VMEM((CHIPS, TOK, D), jnp.bfloat16),
            pltpu.SemaphoreType.DMA((nchunk,)),
            pltpu.SemaphoreType.DMA((8,)),
            pltpu.SemaphoreType.DMA((nchunk,)),
        ],
        compiler_params=pltpu.CompilerParams(vmem_limit_bytes=VMEM_LIMIT),
        cost_estimate=pl.CostEstimate(flops=6_000_000_000, bytes_accessed=40_000_000, transcendentals=0),
        name="experts",
    )(es, g, wi, wo)


def reduce_items(pr):
    row, items, span = D * 2 / 46.5, {}, {}

    def add(name, link, deps, lo, hi):
        span[name] = (lo, hi)
        items[name] = (link, (hi - lo) * row, deps)

    for dz in (4, 3, 5, 2, 6, 1, 7, 0):
        for s in (1, -1):
            add(("A", dz, s), ("x", s), [], *split(0, pr, s))
    for dx in (2, 1, 3, 0):
        for s in (1, -1):
            add(("D", dx, s, 4), ("z", s), [], *split(pr, TOK, s))
    for dz in (4, 3, 5, 2, 6, 1, 7, 0):
        for s in (1, -1):
            add(("B", dz, s), ("x", s), [("A", dz, s)], 0, pr)
    for s in (1, -1):
        for d in (4, 3, 2, 1):
            dz = (s * d) % NZ
            deps = [("B", dz, 1), ("B", dz, -1)] + ([("C", s, d + 1)] if d < 4 else [])
            add(("C", s, d), ("z", s), deps, *(split(0, pr, s) if d == 4 else (0, pr)))
    for dx in (2, 1, 3, 0):
        for s in (1, -1):
            for d in (3, 2, 1):
                add(("D", dx, s, d), ("z", s), [("D", dx, s, d + 1)], pr, TOK)
    for s in (1, -1):
        for d in (2, 1):
            dx = (s * d) % NX
            deps = [("D", dx, 1, 1), ("D", dx, -1, 1)] + ([("E", s, 2)] if d < 2 else [])
            add(("E", s, d), ("x", s), deps, *(split(pr, TOK, s) if d == 2 else (pr, TOK)))
    return items, span


def reduce_kernel(pr, part, out, pv, land, ssem, rsem, lsem):
    y, e, c, x, z = place()
    items, span = reduce_items(pr)
    index, base, top = {}, {}, 0
    for i, name in enumerate(items):
        index[name], base[name] = i, top
        top += span[name][1] - span[name][0]
    for b in range(CHIPS // 4):
        pltpu.make_async_copy(part.at[pl.ds(4 * b, 4)], pv.at[pl.ds(4 * b, 4)], lsem.at[b]).start()
    greet(TORUS)
    for b in range(CHIPS // 4):
        pltpu.make_async_copy(part.at[pl.ds(4 * b, 4)], pv.at[pl.ds(4 * b, 4)], lsem.at[b]).wait()

    def block(name, shift):
        kind, s = name[0], name[2] if name[0] in "ABD" else name[1]
        if kind == "A":
            return chip_at(x, z, s * (2 - shift), name[1])
        if kind == "B":
            return chip_at(x, z, s * (1 - shift), name[1])
        d = name[-1] - shift
        if kind == "C":
            return chip_at(x, z, 0, s * d)
        if kind == "D":
            return chip_at(x, z, name[1], s * d)
        return chip_at(x, z, s * d, 0)

    def copy(name):
        lo, hi = span[name]
        i = index[name]
        return pltpu.make_async_remote_copy(
            src_ref=pv.at[block(name, 0), pl.ds(lo, hi - lo)],
            dst_ref=land.at[pl.ds(base[name], hi - lo)],
            send_sem=ssem.at[i],
            recv_sem=rsem.at[i],
            device_id=neighbour(items[name][0]),
            device_id_type=MESH,
        )

    def fold(name):
        lo, hi = span[name]
        b = block(name, 1)

        def body(i, _):
            to = pl.ds(pl.multiple_of(lo + i * 16, 16), 16)
            src = pl.ds(pl.multiple_of(base[name] + i * 16, 16), 16)
            pv[b, to, :] = (
                pv[b, to, :].astype(jnp.float32) + land[src, :].astype(jnp.float32)
            ).astype(jnp.bfloat16)
            return 0

        lax.fori_loop(0, (hi - lo) // 16, body, 0)

    for op, name in order_of(items):
        if op == "start":
            copy(name).start()
        else:
            copy(name).wait_recv()
            fold(name)
    out[...] = pv[chip_at(x, z, 0, 0)]
    for name in items:
        copy(name).wait_send()


def reduce(pr, part):
    items, span = reduce_items(pr)
    count, rows = len(items), sum(hi - lo for lo, hi in span.values())
    return pl.pallas_call(
        functools.partial(reduce_kernel, pr),
        out_shape=jax.ShapeDtypeStruct((TOK, D), jnp.bfloat16),
        in_specs=[pl.BlockSpec(memory_space=pl.ANY)],
        out_specs=pl.BlockSpec(memory_space=pltpu.VMEM),
        scratch_shapes=[
            pltpu.VMEM((CHIPS, TOK, D), jnp.bfloat16),
            pltpu.VMEM((rows, D), jnp.bfloat16),
            pltpu.SemaphoreType.DMA((count,)),
            pltpu.SemaphoreType.DMA((count,)),
            pltpu.SemaphoreType.DMA((CHIPS // 4,)),
        ],
        compiler_params=pltpu.CompilerParams(
            collective_id=1, has_side_effects=True, vmem_limit_bytes=VMEM_LIMIT
        ),
        cost_estimate=pl.CostEstimate(flops=0, bytes_accessed=200_000_000, transcendentals=0),
        name="reduce",
    )(part)


def tiles_of(array):
    slots, columns = array.shape[0], array.shape[-1]
    rows = array.size // slots // columns
    tiled = array.reshape(slots, rows // 8, 8, columns // 128, 128)
    return tiled.transpose(0, 1, 3, 2, 4).reshape(slots, -1, 8, 128)


def untile(tiles, shape):
    slots, columns = shape[0], shape[-1]
    tiled = tiles.reshape(slots, -1, columns // 128, 8, 128)
    return tiled.transpose(0, 1, 3, 2, 4).reshape(shape)


def on_device(
    tokens, w_in, w_out, moments_in, moments_out, expert_ids, route_weights, old_plan, new_plan
):
    devices = lax.axis_size("exp")
    slots = 2 * devices
    slot_index = jnp.arange(slots, dtype=jnp.int32)
    same_expert = new_plan[:, None] == old_plan[None, :]
    source = jnp.min(jnp.where(same_expert, slot_index[None, :], slots), axis=1)

    state = [w_in, w_out, moments_in, moments_out]
    pooled = jnp.concatenate(
        [tiles_of(a) for a in state] + [jnp.zeros((2, 64 * CHUNK - TILES, 8, 128), jnp.bfloat16)], axis=1
    )
    pooled = pooled.reshape(2, devices, CHUNK * 8, 128).transpose(1, 0, 2, 3)
    spread = lax.all_to_all(pooled, "exp", split_axis=0, concat_axis=0, tiled=True)

    share = route_weights / jnp.sum(route_weights, axis=1, keepdims=True)
    meta = jnp.concatenate(
        [
            expert_ids.T.astype(jnp.bfloat16),
            share.T.astype(jnp.bfloat16),
            jnp.zeros((META, D - 2 * TOK), jnp.bfloat16),
        ],
        axis=1,
    )
    g, gi, go = gather(96, jnp.concatenate([tokens, meta], axis=0), w_in, w_out)

    picked = jnp.take(spread.reshape(slots, CHUNK * 8, 128), source, axis=0)
    landed = lax.all_to_all(
        picked.reshape(devices, 2, CHUNK * 8, 128), "exp", split_axis=0, concat_axis=0, tiled=True
    )

    earlier = (old_plan[:, None] == old_plan[None, :]) & (slot_index[None, :] < slot_index[:, None])
    computes = jnp.where(jnp.any(earlier, axis=1), -1, old_plan)
    es = lax.dynamic_slice(computes, (lax.axis_index("exp") // 2 * 4,), (4,))
    mixed = reduce(96, experts_of(es, g, gi, go))

    tiles = landed.transpose(1, 0, 2, 3).reshape(2, 64 * CHUNK, 8, 128)
    outs, at = [], 0
    for a in state:
        count = a.size // 2 // 1024
        outs.append(untile(tiles[:, at : at + count], a.shape))
        at += count
    return (mixed, *outs)


def solution(mesh):
    return jax.shard_map(
        on_device,
        mesh=mesh,
        in_specs=(
            P(("grp", "exp"), None),
            P("exp", "grp", None),
            P("exp", "grp", None),
            P("exp", None, "grp", None),
            P("exp", None, "grp", None),
            P(("grp", "exp"), None),
            P(("grp", "exp"), None),
            P(),
            P(),
        ),
        out_specs=(
            P(("grp", "exp"), None),
            P("exp", "grp", None),
            P("exp", "grp", None),
            P("exp", None, "grp", None),
            P("exp", None, "grp", None),
        ),
        check_vma=False,
    )
```

```python
import functools
import heapq

import jax
import jax.numpy as jnp
from jax import lax
from jax.experimental import pallas as pl
from jax.experimental.pallas import tpu as pltpu
from jax.sharding import PartitionSpec as P

TOP = 8
TOK = 128
D = 1024
H = 384
NX, NZ, NY = 4, 8, 8
META = 8
ROWS = TOK + META
CAP = 16
CHIPS = NX * NZ
MESH = pl.DeviceIdType.MESH
VMEM_LIMIT = 62 * 1024 * 1024
TILES = 432
CHUNK = 7
GATHER_ROWS = 104
REDUCE_ROWS = 96


def order_of(items):
    free, heap, started, arrived, ops = {}, [], set(), set(), []

    def start_ready(now):
        for name, (link, size, deps) in items.items():
            if name not in started and all(d in arrived for d in deps):
                begin = max(now, free.get(link, 0.0))
                free[link] = begin + size
                heapq.heappush(heap, (free[link] + (600.0 if link[0] != "c" else 100.0), len(started), name))
                started.add(name)
                ops.append(("start", name))

    start_ready(0.0)
    while heap:
        now, _, name = heapq.heappop(heap)
        arrived.add(name)
        ops.append(("wait", name))
        start_ready(now)
    return ops


def split(lo, hi, s):
    mid = lo + ((hi - lo) // 2 + 7) // 8 * 8
    return (lo, mid) if s > 0 else (mid, hi)


def place():
    y = lax.axis_index("grp")
    e = lax.axis_index("exp")
    c = lax.rem(e, 2)
    r = e // 2
    return y, e, c, r // NZ, lax.rem(r, NZ)


def chip_at(x, z, dx, dz):
    return lax.rem(x + dx + NX, NX) * NZ + lax.rem(z + dz + NZ, NZ)


def neighbour(link):
    y, e, c, x, z = place()
    axis, s = link
    if axis == "x":
        return (y, 2 * chip_at(x, z, s, 0) + c)
    if axis == "z":
        return (y, 2 * chip_at(x, z, 0, s) + c)
    if axis == "y":
        return (lax.rem(y + s + NY, NY), e)
    return (y, e + 1 - 2 * c)


def greet(links):
    barrier = pltpu.get_barrier_semaphore()
    for link in links:
        pl.semaphore_signal(barrier, inc=1, device_id=neighbour(link), device_id_type=MESH)
    pl.semaphore_wait(barrier, len(links))


TORUS = (("x", 1), ("x", -1), ("z", 1), ("z", -1))


def gather_items(pr):
    row, items = D * 2 / 46.5, {}

    def rows_of(name):
        lo, hi = (0, pr) if name[0][0] == "P" else (pr, ROWS)
        half = name[-1] == (4 if name[0][1] == "Z" else 2)
        return split(lo, hi, name[-2]) if half else (lo, hi)

    def add(name, link, deps):
        lo, hi = rows_of(name)
        items[name] = (link, (hi - lo) * row, deps)

    for s in (1, -1):
        for d in (1, 2, 3, 4):
            add(("PZ", s, d), ("z", s), [("PZ", s, d - 1)] if d > 1 else [])
        for d in (1, 2):
            add(("QX", s, d), ("x", s), [("QX", s, d - 1)] if d > 1 else [])
    for s in (1, -1):
        for d in (1, 2, 3, 4):
            dep = lambda k: [(k, s, d - 1)] if d > 1 else []
            part = 0.5 if d == 4 else 1.0
            items[("WI", s, d)] = (("y", s), part * 2 * 128 * 768 * 2 / 46.5, dep("WI"))
            items[("WO", s, d)] = (("y", s), part * 2 * 48 * 1024 * 2 / 46.5, dep("WO"))
    for dz in (0, 1, 7, 2, 6, 3, 5, 4):
        for s in (1, -1):
            for d in (1, 2):
                if d == 2:
                    deps = [("PX", dz, s, 1)]
                elif dz == 0:
                    deps = []
                elif dz == 4:
                    deps = [("PZ", 1, 4), ("PZ", -1, 4)]
                else:
                    deps = [("PZ", -1, dz)] if dz < 4 else [("PZ", 1, 8 - dz)]
                add(("PX", dz, s, d), ("x", s), deps)
    for dx in (0, 1, 3, 2):
        for s in (1, -1):
            for d in (1, 2, 3, 4):
                if d > 1:
                    deps = [("QZ", dx, s, d - 1)]
                elif dx == 0:
                    deps = []
                elif dx == 2:
                    deps = [("QX", 1, 2), ("QX", -1, 2)]
                else:
                    deps = [("QX", -1, 1)] if dx == 1 else [("QX", 1, 1)]
                add(("QZ", dx, s, d), ("z", s), deps)
    for dy in range(NY):
        for k, size in (("WI", 393216), ("WO", 196608)):
            if dy == 0:
                deps = []
            elif dy == 4:
                deps = [(k, 1, 4), (k, -1, 4)]
            else:
                deps = [(k, -1, dy)] if dy < 4 else [(k, 1, 8 - dy)]
            items[("S" + k, dy)] = (("c", 0), size / 300.0, deps)
    return items, rows_of


def gather_kernel(pr, xt, wi, wo, g, gi, go, ssem, rsem, lsem):
    y, e, c, x, z = place()
    items, rows_of = gather_items(pr)
    index = {name: i for i, name in enumerate(items)}
    greet(TORUS + (("y", 1), ("y", -1), ("c", 0)))
    own = chip_at(x, z, 0, 0)
    span_i, span_o = wi.shape[1], wo.shape[1]

    def weights(k, dy, slots, core):
        ref, span = (gi, span_i) if k == "WI" else (go, span_o)
        at = pl.multiple_of(lax.rem(y + dy + NY, NY) * span, span)
        return ref.at[pl.ds(2 * core + slots[0], slots[1]), pl.ds(at, span)]

    def ends(name, shift):
        kind = name[0]
        if kind[0] == "S":
            k, dy = kind[1:], name[1]
            core = c if shift else 1 - c
            dst = weights(k, dy, (0, 2), core)
            return ((wi if k == "WI" else wo) if dy == 0 else dst), dst
        if kind[0] == "W":
            s, d = name[1:]
            slots = (0, 2) if d < 4 else ((0, 1) if s > 0 else (1, 1))
            dst = weights(kind, -s * (d - shift), slots, c)
            return ((wi if kind == "WI" else wo) if d == 1 else dst), dst
        lo, hi = rows_of(name)
        s, d = name[-2:]
        off = -s * (d - shift)
        if kind == "PZ":
            dx, dz = 0, off
        elif kind == "QX":
            dx, dz = off, 0
        elif kind == "PX":
            dx, dz = off, name[1]
        else:
            dx, dz = name[1], off
        dst = g.at[chip_at(x, z, dx, dz), pl.ds(lo, hi - lo)]
        mine = shift == 1 and dx % NX == 0 and dz % NZ == 0
        return (xt.at[pl.ds(lo, hi - lo)] if mine else dst), dst

    def copy(name, shift):
        src, dst = ends(name, shift)
        i = index[name]
        return pltpu.make_async_remote_copy(
            src_ref=src if shift else dst,
            dst_ref=dst,
            send_sem=ssem.at[i],
            recv_sem=rsem.at[i],
            device_id=neighbour(items[name][0]),
            device_id_type=MESH,
        )

    local = [
        pltpu.make_async_copy(xt, g.at[own], lsem.at[0]),
        pltpu.make_async_copy(wi, weights("WI", 0, (0, 2), c), lsem.at[1]),
        pltpu.make_async_copy(wo, weights("WO", 0, (0, 2), c), lsem.at[2]),
    ]
    for name_op in order_of(items):
        op, name = name_op
        if op == "start":
            copy(name, 1).start()
        else:
            copy(name, 0).wait_recv()
        if local and op == "wait":
            for item in local:
                item.start()
            done, local = local, []
    for item in done:
        item.wait()
    for name in items:
        copy(name, 1).wait_send()


def gather(pr, xt, wi, wo):
    count = len(gather_items(pr)[0])
    any_space = pl.BlockSpec(memory_space=pl.ANY)
    vmem = pl.BlockSpec(memory_space=pltpu.VMEM)
    return pl.pallas_call(
        functools.partial(gather_kernel, pr),
        out_shape=(
            jax.ShapeDtypeStruct((CHIPS, ROWS, D), jnp.bfloat16),
            jax.ShapeDtypeStruct((4, D, 2 * H), jnp.bfloat16),
            jax.ShapeDtypeStruct((4, H, D), jnp.bfloat16),
        ),
        in_specs=[vmem] * 3,
        out_specs=(any_space,) * 3,
        scratch_shapes=[
            pltpu.SemaphoreType.DMA((count,)),
            pltpu.SemaphoreType.DMA((count,)),
            pltpu.SemaphoreType.DMA((3,)),
        ],
        compiler_params=pltpu.CompilerParams(
            collective_id=0, has_side_effects=True, vmem_limit_bytes=VMEM_LIMIT
        ),
        cost_estimate=pl.CostEstimate(flops=0, bytes_accessed=200_000_000, transcendentals=0),
        name="gather",
    )(xt, wi, wo)


STEP = 8


def expert_kernel(es, g, wi, wo, part, gv, wiv, wov, xs, ys, cnt, wgt, rank, sel, outv, isem, wsem, osem):
    nchunk = CHIPS // STEP
    for n in range(nchunk):
        pltpu.make_async_copy(g.at[pl.ds(n * STEP, STEP)], gv.at[pl.ds(n * STEP, STEP)], isem.at[n]).start()
    for j in range(4):
        pltpu.make_async_copy(wi.at[j], wiv.at[j], wsem.at[j]).start()
        pltpu.make_async_copy(wo.at[j], wov.at[j], wsem.at[4 + j]).start()
    tri = (
        lax.broadcasted_iota(jnp.int32, (TOK, TOK), 0) <= lax.broadcasted_iota(jnp.int32, (TOK, TOK), 1)
    ).astype(jnp.bfloat16)
    line = lax.broadcasted_iota(jnp.int32, (CAP, TOK), 0).astype(jnp.float32)
    experts = [es[j].astype(jnp.float32) for j in range(4)]
    for n in range(nchunk):
        pltpu.make_async_copy(
            g.at[pl.ds(n * STEP, STEP)], gv.at[pl.ds(n * STEP, STEP)], isem.at[n]
        ).wait()

        def count(i, _):
            b = n * STEP + i
            meta = gv[b, TOK:ROWS, 0 : 3 * TOK].astype(jnp.float32)
            ids, share = meta[:, 0:TOK], meta[:, TOK : 2 * TOK] + meta[:, 2 * TOK :]
            named = [ids == experts[j] for j in range(4)]
            ones = [jnp.sum(jnp.where(m, 1.0, 0.0), axis=0, keepdims=True) for m in named]
            held = [jnp.sum(jnp.where(m, share, 0.0), axis=0, keepdims=True) for m in named]
            rows = pl.ds(pl.multiple_of(b * 8, 8), 8)
            cnt[rows, :] = jnp.concatenate(ones + ones, axis=0)
            wgt[rows, :] = jnp.concatenate(held + held, axis=0)
            return 0

        lax.fori_loop(0, STEP, count, 0)
        rows = pl.ds(n * STEP * 8, STEP * 8)
        chosen = cnt[rows, :]
        upto = jnp.dot(chosen.astype(jnp.bfloat16), tri, preferred_element_type=jnp.float32)
        rank[rows, :] = jnp.where(chosen > 0.5, upto - 1.0, -1.0)

        def pick(i, _):
            b = n * STEP + i
            rows = pl.ds(pl.multiple_of(b * 8, 8), 8)
            place8, held8 = rank[rows, :], wgt[rows, :]
            hit = [line == place8[j : j + 1, :] for j in range(4)]
            onehot = jnp.concatenate([jnp.where(m, 1.0, 0.0) for m in hit], axis=0)
            weight = jnp.concatenate(
                [jnp.where(hit[j], held8[j : j + 1, :], 0.0) for j in range(4)], axis=0
            )
            high = weight.astype(jnp.bfloat16)
            sel[b, 0 : 4 * CAP, :] = high
            sel[b, 4 * CAP :, :] = (weight - high.astype(jnp.float32)).astype(jnp.bfloat16)
            got = jnp.dot(
                onehot.astype(jnp.bfloat16), gv[b, 0:TOK, :], preferred_element_type=jnp.float32
            ).astype(jnp.bfloat16)
            at = pl.ds(pl.multiple_of(b * CAP, CAP), CAP)
            for j in range(4):
                xs[j, at, :] = got[j * CAP : (j + 1) * CAP, :]
            return 0

        lax.fori_loop(0, STEP, pick, 0, unroll=2)
    for j in range(4):
        pltpu.make_async_copy(wi.at[j], wiv.at[j], wsem.at[j]).wait()
        pltpu.make_async_copy(wo.at[j], wov.at[j], wsem.at[4 + j]).wait()

    def mlp(i, _):
        j, at = i // 2, pl.ds(pl.multiple_of(lax.rem(i, 2) * 256, 256), 256)
        both = jnp.dot(xs[j, at, :], wiv[j], preferred_element_type=jnp.float32)
        hidden = (jax.nn.silu(both[:, :H]) * both[:, H:]).astype(jnp.bfloat16)
        ys[j, at, :] = jnp.dot(hidden, wov[j], preferred_element_type=jnp.float32).astype(jnp.bfloat16)
        return 0

    lax.fori_loop(0, 8, mlp, 0)
    for n in range(nchunk):

        def spread(i, _):
            b = n * STEP + i
            at = pl.ds(pl.multiple_of(b * CAP, CAP), CAP)
            rows = jnp.concatenate([ys[j, at, :] for j in range(4)] * 2, axis=0)
            outv[b] = lax.dot_general(
                sel[b], rows, (((0,), (0,)), ((), ())), preferred_element_type=jnp.float32
            ).astype(jnp.bfloat16)
            return 0

        lax.fori_loop(0, STEP, spread, 0, unroll=2)
        pltpu.make_async_copy(outv.at[pl.ds(n * STEP, STEP)], part.at[pl.ds(n * STEP, STEP)], osem.at[n]).start()
    for n in range(nchunk):
        pltpu.make_async_copy(
            outv.at[pl.ds(n * STEP, STEP)], part.at[pl.ds(n * STEP, STEP)], osem.at[n]
        ).wait()


def experts_of(es, g, wi, wo):
    any_space = pl.BlockSpec(memory_space=pl.ANY)
    nchunk = CHIPS // STEP
    return pl.pallas_call(
        expert_kernel,
        out_shape=jax.ShapeDtypeStruct((CHIPS, TOK, D), jnp.bfloat16),
        in_specs=[pl.BlockSpec(memory_space=pltpu.SMEM)] + [any_space] * 3,
        out_specs=any_space,
        scratch_shapes=[
            pltpu.VMEM((CHIPS, ROWS, D), jnp.bfloat16),
            pltpu.VMEM((4, D, 2 * H), jnp.bfloat16),
            pltpu.VMEM((4, H, D), jnp.bfloat16),
            pltpu.VMEM((4, CHIPS * CAP, D), jnp.bfloat16),
            pltpu.VMEM((4, CHIPS * CAP, D), jnp.bfloat16),
            pltpu.VMEM((CHIPS * 8, TOK), jnp.float32),
            pltpu.VMEM((CHIPS * 8, TOK), jnp.float32),
            pltpu.VMEM((CHIPS * 8, TOK), jnp.float32),
            pltpu.VMEM((CHIPS, 8 * CAP, TOK), jnp.bfloat16),
            pltpu.VMEM((CHIPS, TOK, D), jnp.bfloat16),
            pltpu.SemaphoreType.DMA((nchunk,)),
            pltpu.SemaphoreType.DMA((8,)),
            pltpu.SemaphoreType.DMA((nchunk,)),
        ],
        compiler_params=pltpu.CompilerParams(vmem_limit_bytes=VMEM_LIMIT),
        cost_estimate=pl.CostEstimate(flops=6_000_000_000, bytes_accessed=40_000_000, transcendentals=0),
        name="experts",
    )(es, g, wi, wo)


def reduce_items(pr):
    row, items, span = D * 2 / 46.5, {}, {}

    def add(name, link, deps, lo, hi):
        span[name] = (lo, hi)
        items[name] = (link, (hi - lo) * row, deps)

    for dz in (4, 3, 5, 2, 6, 1, 7, 0):
        for s in (1, -1):
            add(("A", dz, s), ("x", s), [], *split(0, pr, s))
    for dx in (2, 1, 3, 0):
        for s in (1, -1):
            add(("D", dx, s, 4), ("z", s), [], *split(pr, TOK, s))
    for dz in (4, 3, 5, 2, 6, 1, 7, 0):
        for s in (1, -1):
            add(("B", dz, s), ("x", s), [("A", dz, s)], 0, pr)
    for s in (1, -1):
        for d in (4, 3, 2, 1):
            dz = (s * d) % NZ
            deps = [("B", dz, 1), ("B", dz, -1)] + ([("C", s, d + 1)] if d < 4 else [])
            add(("C", s, d), ("z", s), deps, *(split(0, pr, s) if d == 4 else (0, pr)))
    for dx in (2, 1, 3, 0):
        for s in (1, -1):
            for d in (3, 2, 1):
                add(("D", dx, s, d), ("z", s), [("D", dx, s, d + 1)], pr, TOK)
    for s in (1, -1):
        for d in (2, 1):
            dx = (s * d) % NX
            deps = [("D", dx, 1, 1), ("D", dx, -1, 1)] + ([("E", s, 2)] if d < 2 else [])
            add(("E", s, d), ("x", s), deps, *(split(pr, TOK, s) if d == 2 else (pr, TOK)))
    return items, span


def reduce_kernel(pr, part, out, pv, land, ssem, rsem, lsem):
    y, e, c, x, z = place()
    items, span = reduce_items(pr)
    index, base, top = {}, {}, 0
    for i, name in enumerate(items):
        index[name], base[name] = i, top
        top += span[name][1] - span[name][0]
    for b in range(CHIPS // 4):
        pltpu.make_async_copy(part.at[pl.ds(4 * b, 4)], pv.at[pl.ds(4 * b, 4)], lsem.at[b]).start()
    greet(TORUS)
    for b in range(CHIPS // 4):
        pltpu.make_async_copy(part.at[pl.ds(4 * b, 4)], pv.at[pl.ds(4 * b, 4)], lsem.at[b]).wait()

    def block(name, shift):
        kind, s = name[0], name[2] if name[0] in "ABD" else name[1]
        if kind == "A":
            return chip_at(x, z, s * (2 - shift), name[1])
        if kind == "B":
            return chip_at(x, z, s * (1 - shift), name[1])
        d = name[-1] - shift
        if kind == "C":
            return chip_at(x, z, 0, s * d)
        if kind == "D":
            return chip_at(x, z, name[1], s * d)
        return chip_at(x, z, s * d, 0)

    def copy(name):
        lo, hi = span[name]
        i = index[name]
        return pltpu.make_async_remote_copy(
            src_ref=pv.at[block(name, 0), pl.ds(lo, hi - lo)],
            dst_ref=land.at[pl.ds(base[name], hi - lo)],
            send_sem=ssem.at[i],
            recv_sem=rsem.at[i],
            device_id=neighbour(items[name][0]),
            device_id_type=MESH,
        )

    def fold(name):
        lo, hi = span[name]
        b = block(name, 1)

        def body(i, _):
            to = pl.ds(pl.multiple_of(lo + i * 16, 16), 16)
            src = pl.ds(pl.multiple_of(base[name] + i * 16, 16), 16)
            pv[b, to, :] = (
                pv[b, to, :].astype(jnp.float32) + land[src, :].astype(jnp.float32)
            ).astype(jnp.bfloat16)
            return 0

        lax.fori_loop(0, (hi - lo) // 16, body, 0)

    for op, name in order_of(items):
        if op == "start":
            copy(name).start()
        else:
            copy(name).wait_recv()
            fold(name)
    out[...] = pv[chip_at(x, z, 0, 0)]
    for name in items:
        copy(name).wait_send()


def reduce(pr, part):
    items, span = reduce_items(pr)
    count, rows = len(items), sum(hi - lo for lo, hi in span.values())
    return pl.pallas_call(
        functools.partial(reduce_kernel, pr),
        out_shape=jax.ShapeDtypeStruct((TOK, D), jnp.bfloat16),
        in_specs=[pl.BlockSpec(memory_space=pl.ANY)],
        out_specs=pl.BlockSpec(memory_space=pltpu.VMEM),
        scratch_shapes=[
            pltpu.VMEM((CHIPS, TOK, D), jnp.bfloat16),
            pltpu.VMEM((rows, D), jnp.bfloat16),
            pltpu.SemaphoreType.DMA((count,)),
            pltpu.SemaphoreType.DMA((count,)),
            pltpu.SemaphoreType.DMA((CHIPS // 4,)),
        ],
        compiler_params=pltpu.CompilerParams(
            collective_id=1, has_side_effects=True, vmem_limit_bytes=VMEM_LIMIT
        ),
        cost_estimate=pl.CostEstimate(flops=0, bytes_accessed=200_000_000, transcendentals=0),
        name="reduce",
    )(part)


def tiles_of(array):
    slots, columns = array.shape[0], array.shape[-1]
    rows = array.size // slots // columns
    tiled = array.reshape(slots, rows // 8, 8, columns // 128, 128)
    return tiled.transpose(0, 1, 3, 2, 4).reshape(slots, -1, 8, 128)


def untile(tiles, shape):
    slots, columns = shape[0], shape[-1]
    tiled = tiles.reshape(slots, -1, columns // 128, 8, 128)
    return tiled.transpose(0, 1, 3, 2, 4).reshape(shape)


def on_device(
    tokens, w_in, w_out, moments_in, moments_out, expert_ids, route_weights, old_plan, new_plan
):
    devices = lax.axis_size("exp")
    slots = 2 * devices
    slot_index = jnp.arange(slots, dtype=jnp.int32)
    same_expert = new_plan[:, None] == old_plan[None, :]
    source = jnp.min(jnp.where(same_expert, slot_index[None, :], slots), axis=1)

    state = [w_in, w_out, moments_in, moments_out]
    pooled = jnp.concatenate(
        [tiles_of(a) for a in state] + [jnp.zeros((2, 64 * CHUNK - TILES, 8, 128), jnp.bfloat16)], axis=1
    )
    pooled = pooled.reshape(2, devices, CHUNK * 8, 128).transpose(1, 0, 2, 3)
    share = route_weights / jnp.sum(route_weights, axis=1, keepdims=True)
    meta = jnp.concatenate(
        [
            expert_ids.T.astype(jnp.bfloat16),
            share.T.astype(jnp.bfloat16),
            (share.T - lax.reduce_precision(share.T, 8, 7)).astype(jnp.bfloat16),
            jnp.zeros((META, D - 3 * TOK), jnp.bfloat16),
        ],
        axis=1,
    )
    sent, pooled_in = lax.optimization_barrier((jnp.concatenate([tokens, meta], axis=0), pooled))
    spread = lax.all_to_all(pooled_in, "exp", split_axis=0, concat_axis=0, tiled=True)
    g, gi, go = gather(GATHER_ROWS, sent, w_in, w_out)
    spread, g = lax.optimization_barrier((spread, g))

    picked = jnp.take(spread.reshape(slots, CHUNK * 8, 128), source, axis=0, mode="clip")
    picked, g = lax.optimization_barrier((picked, g))
    landed = lax.all_to_all(
        picked.reshape(devices, 2, CHUNK * 8, 128), "exp", split_axis=0, concat_axis=0, tiled=True
    )

    earlier = (old_plan[:, None] == old_plan[None, :]) & (slot_index[None, :] < slot_index[:, None])
    computes = jnp.where(jnp.any(earlier, axis=1), -1, old_plan)
    es = lax.dynamic_slice(computes, (lax.axis_index("exp") // 2 * 4,), (4,))
    mixed = reduce(REDUCE_ROWS, experts_of(es, g, gi, go))

    tiles = landed.transpose(1, 0, 2, 3).reshape(2, 64 * CHUNK, 8, 128)
    outs, at = [], 0
    for a in state:
        count = a.size // 2 // 1024
        outs.append(untile(tiles[:, at : at + count], a.shape))
        at += count
    return (mixed, *outs)


def solution(mesh):
    return jax.shard_map(
        on_device,
        mesh=mesh,
        in_specs=(
            P(("grp", "exp"), None),
            P("exp", "grp", None),
            P("exp", "grp", None),
            P("exp", None, "grp", None),
            P("exp", None, "grp", None),
            P(("grp", "exp"), None),
            P(("grp", "exp"), None),
            P(),
            P(),
        ),
        out_specs=(
            P(("grp", "exp"), None),
            P("exp", "grp", None),
            P("exp", "grp", None),
            P("exp", None, "grp", None),
            P("exp", None, "grp", None),
        ),
        check_vma=False,
    )
```

```python
import functools
import heapq

import jax
import jax.numpy as jnp
from jax import lax
from jax.experimental import pallas as pl
from jax.experimental.pallas import tpu as pltpu
from jax.sharding import PartitionSpec as P

TOP = 8
TOK = 128
D = 1024
H = 384
NX, NZ, NY = 4, 8, 8
META = 8
ROWS = TOK + META
CAP = 16
CHIPS = NX * NZ
MESH = pl.DeviceIdType.MESH
VMEM_LIMIT = 63 * 1024 * 1024
TILES = 432
CHUNK = 14
PIECE = CHUNK * 8
GATHER_ROWS = 104
REDUCE_ROWS = 96
AHEAD = 6000.0
RATE = 43.3
HOP = 1500.0
GROUPS = (0, 1, 7, 2, 6, 3, 5, 4)
SPREAD = (4, 3, 5, 2, 6, 1, 7, 0)
TORUS = (("x", 1), ("x", -1), ("z", 1), ("z", -1))
LINKS = TORUS + (("y", 1), ("y", -1), ("c", 0))


def order_of(items):
    after, missing, tail = {n: [] for n in items}, {}, {}
    for name, (_, _, deps) in items.items():
        missing[name] = len(set(deps))
        for d in set(deps):
            after[d].append(name)

    def lag(name):
        axis = items[name][0][0]
        return 0.0 if axis == "t" else 500.0 if axis == "c" else HOP

    def measure(name):
        if name not in tail:
            later = max([measure(n) for n in after[name]], default=0.0)
            tail[name] = items[name][1] + lag(name) + later
        return tail[name]

    place_of = {name: i for i, name in enumerate(items)}
    ready = {item[0][:2]: [] for item in items.values()}
    free, heap, ops, busy = dict.fromkeys(ready, 0.0), [], [], [False]

    def push(name):
        heapq.heappush(ready[items[name][0][:2]], (-measure(name), place_of[name], name))

    def issue(now):
        for link, queue in ready.items():
            while queue and (not busy[0] if link[0] == "t" else free[link] - now < AHEAD):
                name = heapq.heappop(queue)[2]
                busy[0] = busy[0] or link[0] == "t"
                free[link] = max(now, free[link]) + items[name][1]
                heapq.heappush(heap, (free[link] + lag(name), len(ops), name))
                ops.append(("start", name))

    for name in items:
        if not missing[name]:
            push(name)
    now = 0.0
    issue(now)
    while heap:
        now, _, name = heapq.heappop(heap)
        if items[name][0][0] == "t":
            busy[0] = False
        else:
            ops.append(("wait", name))
        for later in after[name]:
            missing[later] -= 1
            if not missing[later]:
                push(later)
        issue(now)
    return ops, now


def split(lo, hi, s):
    mid = lo + ((hi - lo) // 2 + 7) // 8 * 8
    return (lo, mid) if s > 0 else (mid, hi)


def ring(kind, at):
    size = NX if kind[0][1] == "X" else NZ
    at, half = at % size, size // 2
    if at == 0:
        return []
    if at == half:
        return [kind + (1, half), kind + (-1, half)]
    return [kind + (-1, at)] if at < half else [kind + (1, size - at)]


def plan(stage):
    items, span = {}, {}

    def copy(name, link, count, deps):
        items[name] = (link, count / (600.0 if link[0] == "c" else RATE), deps)

    def rows(name, link, lo, hi, deps):
        span[name] = (lo, hi)
        copy(name, link, (hi - lo) * D * 2, deps)

    def step(name, time, deps):
        items[name] = (("t", 0), time, deps)

    pr = GATHER_ROWS
    for s in (1, -1):
        for d in (1, 2, 3, 4):
            lo, hi = split(0, pr, s) if d == 4 else (0, pr)
            rows(("PZ", s, d), ("z", s), lo, hi, [("PZ", s, d - 1)] if d > 1 else [])
        for d in (1, 2):
            lo, hi = split(pr, ROWS, s) if d == 2 else (pr, ROWS)
            rows(("QX", s, d), ("x", s), lo, hi, [("QX", s, 1)] if d > 1 else [])
    for s in (1, -1):
        for d in (1, 2, 3, 4):
            for kind, count in (("WI", 393216), ("WO", 196608)):
                deps = [(kind, s, d - 1)] if d > 1 else []
                copy((kind, s, d), ("y", s), count // (2 if d == 4 else 1), deps)
    for dz in GROUPS:
        for s in (1, -1):
            rows(("PX", dz, s, 1), ("x", s), 0, pr, ring(("PZ",), dz))
            rows(("PX", dz, s, 2), ("x", s), *split(0, pr, s), [("PX", dz, s, 1)])
    for dx in (0, 1, 3, 2):
        for s in (1, -1):
            for d in (1, 2, 3, 4):
                lo, hi = split(pr, ROWS, s) if d == 4 else (pr, ROWS)
                deps = [("QZ", dx, s, d - 1)] if d > 1 else ring(("QX",), dx)
                rows(("QZ", dx, s, d), ("z", s), lo, hi, deps)
    weights = []
    for dy in range(NY):
        for kind, count in (("WI", 393216), ("WO", 196608)):
            copy(("S" + kind, dy), ("c", 0), count, ring((kind + "Y",), dy) and [
                (kind,) + k[1:] for k in ring((kind + "Y",), dy)
            ])
            weights += [("S" + kind, dy)] + items[("S" + kind, dy)][2]

    piece = 2 * PIECE * 128 * 2

    def exchange(tag, after):
        for s in (1, -1):
            copy((tag + "X", s, 2, 1), ("x", s), 4 * piece, after)
            copy((tag + "X", s, 1, 1), ("x", s), 8 * piece, after)
            copy((tag + "X", s, 2, 2), ("x", s), 4 * piece, [(tag + "X", s, 2, 1)])
        ends = [(tag + "X", s, d, d) for s in (1, -1) for d in (1, 2)]
        step(("own", tag), 800.0, ends + after)
        for h in (1, 2, 3, 4):
            for d in (4, 3, 2, 1):
                for s in (1, -1):
                    if d >= h:
                        deps = [(tag + "Z", s, d, h - 1)] if h > 1 else [("own", tag)]
                        copy((tag + "Z", s, d, h), ("z", s), (2 if d == 4 else 4) * piece, deps)
        return [(tag + "Z", s, d, d) for s in (1, -1) for d in (1, 2, 3, 4)]

    ends = exchange("U", [])
    for dz in range(NZ):
        deps = [k + (k[2],) for k in ring(("UZ",), dz)]
        copy(("SU", dz), ("c", 0), 4 * piece, deps or [("own", "U")])

    for dz in SPREAD:
        step(("sum", dz), 300.0, [])

    pr = REDUCE_ROWS

    def fold(name, dz):
        step(("fold", name), 60.0 + 3.0 * (span[name][1] - span[name][0]), [name, ("sum", dz % NZ)])

    for dz in SPREAD:
        for s in (1, -1):
            rows(("A", dz, s), ("x", s), *split(0, pr, s), [("sum", dz)])
            fold(("A", dz, s), dz)
        if dz == 4:
            for dx in (2, 1, 3, 0):
                for s in (1, -1):
                    rows(("D", dx, s, 4), ("z", s), *split(pr, TOK, s), [("sum", 4)])
                    fold(("D", dx, s, 4), 3 * s)
    for dx in (2, 1, 3, 0):
        for s in (1, -1):
            for d in (3, 2, 1):
                deps = [("fold", ("D", dx, s, d + 1)), ("sum", (s * d) % NZ)]
                rows(("D", dx, s, d), ("z", s), pr, TOK, deps)
                fold(("D", dx, s, d), s * (d - 1))
    for s in (1, -1):
        for d in (2, 1):
            dx = (s * d) % NX
            deps = [("fold", ("D", dx, 1, 1)), ("fold", ("D", dx, -1, 1))]
            deps += [("fold", ("E", s, 2))] if d < 2 else []
            rows(("E", s, d), ("x", s), *(split(pr, TOK, s) if d == 2 else (pr, TOK)), deps)
            fold(("E", s, d), 0)
    for dz in SPREAD:
        for s in (1, -1):
            rows(("B", dz, s), ("x", s), 0, pr, [("fold", ("A", dz, s)), ("sum", dz)])
            fold(("B", dz, s), dz)
    for s in (1, -1):
        for d in (4, 3, 2, 1):
            dz = (s * d) % NZ
            deps = [("fold", ("B", dz, 1)), ("fold", ("B", dz, -1))]
            deps += [("fold", ("C", s, d + 1))] if d < 4 else []
            rows(("C", s, d), ("z", s), *(split(0, pr, s) if d == 4 else (0, pr)), deps)
            fold(("C", s, d), s * (d - 1))
    first = {
        name: item for name, item in items.items()
        if name[0][0] in "PQWSU" or name == ("own", "U")
    }
    first = {n: (link, t, [d for d in deps if d in first]) for n, (link, t, deps) in first.items()}
    rest = {n: item for n, item in items.items() if n not in first}
    rest = {n: (link, t, [d for d in deps if d in rest]) for n, (link, t, deps) in rest.items()}
    return first if stage == 0 else rest, span


def gather_kernel(xt, wi, wo, pool, g, gi, go, store, xb, zt, hop, ssem, rsem, lsem):
    run(0, xt, wi, wo, pool, None, g, gi, go, None, None, store, xb, zt, hop, ssem, rsem, lsem, None)


def reduce_kernel(psrc, out, part, land, ssem, rsem, lsem):
    run(1, None, None, None, None, out, None, None, None, part, land, None, None, None, None,
        ssem, rsem, lsem, psrc)


def run(
    stage, xt, wi, wo, pool, out, g, gi, go, part, land, store, xb, zt, hop, ssem, rsem, lsem, psrc,
):
    y = lax.axis_index("grp")
    e = lax.axis_index("exp")
    c = lax.rem(e, 2)
    x, z = e // (2 * NZ), lax.rem(e // 2, NZ)
    xat = [x] + [lax.rem(x + d, NX) for d in range(1, NX)]
    zat = [z] + [lax.rem(z + d, NZ) for d in range(1, NZ)]
    yat = [y] + [lax.rem(y + d, NY) for d in range(1, NY)]
    chips = [[xat[dx] * NZ + zat[dz] for dz in range(NZ)] for dx in range(NX)]
    peer = {("c", 0): (y, e + 1 - 2 * c)}
    for s in (1, -1):
        peer[("x", s)] = (y, 2 * chips[s % NX][0] + c)
        peer[("z", s)] = (y, 2 * chips[0][s % NZ] + c)
        peer[("y", s)] = (yat[s % NY], e)
    span_at = {
        "I": [pl.multiple_of(yat[d] * 128, 128) for d in range(NY)],
        "O": [pl.multiple_of(yat[d] * 48, 16) for d in range(NY)],
    }
    other = 1 - c
    chips_row = [xat[dx] * NZ for dx in range(NX)]
    first_slot = [2 * c, 2 * c + 1, 2 * (1 - c)]

    def chip_at(dx, dz):
        return chips[dx % NX][dz % NZ]

    items, span = plan(stage)
    order, _ = order_of(items)
    copies = [name for name, item in items.items() if item[0][0] != "t"]
    index = {name: i for i, name in enumerate(copies)}
    base, top = {}, 0
    for name in copies:
        if name[0] in ("A", "B", "C", "D", "E"):
            base[name] = top
            top += span[name][1] - span[name][0]
    transit, top = {}, {"U": 0, "V": 0}
    for name in copies:
        if name[0] in ("UZ", "VZ") and name[2] != name[3]:
            transit[name] = top[name[0][0]]
            top[name[0][0]] += 2 if name[2] == 4 else 4
    hop_x = {("U", 1): 0, ("U", -1): 1, ("V", 1): 0, ("V", -1): 1}

    own = chip_at(0, 0)
    def weights(kind, dy, slots, mine):
        ref, size = (gi, 128) if kind == "WI" else (go, 48)
        first = first_slot[slots[0]] if mine else first_slot[2]
        return ref.at[pl.ds(first, slots[1]), pl.ds(span_at[kind[1]][dy % NY], size)]

    links = LINKS if stage == 0 else TORUS
    pending = {}
    if stage == 0:
        pending["last"] = [
            pltpu.make_async_copy(xt, g.at[own], lsem.at[0]),
            pltpu.make_async_copy(wi, weights("WI", 0, (0, 2), 1), lsem.at[1]),
            pltpu.make_async_copy(wo, weights("WO", 0, (0, 2), 1), lsem.at[2]),
        ]
        pending["own", "U"] = [pltpu.make_async_copy(pool.at[pl.ds(chips_row[0], NZ)], xb.at[x], lsem.at[3])]
    else:
        for n, dz in enumerate(SPREAD):
            pending["sum", dz] = [
                pltpu.make_async_copy(psrc.at[chip_at(dx, dz)], part.at[chip_at(dx, dz)], lsem.at[NX * n + dx])
                for dx in range(NX)
            ]
    for group in pending.values():
        for item in group:
            item.start()
    barrier = pltpu.get_barrier_semaphore()
    for link in links:
        pl.semaphore_signal(barrier, inc=1, device_id=peer[link], device_id_type=MESH)
    pl.semaphore_wait(barrier, len(links))

    def block(name, shift):
        kind, s = name[0], name[2] if name[0] in "ABD" else name[1]
        if kind == "A":
            return chip_at(s * (2 - shift), name[1])
        if kind == "B":
            return chip_at(s * (1 - shift), name[1])
        d = name[-1] - shift
        if kind == "C":
            return chip_at(0, s * d)
        if kind == "D":
            return chip_at(name[1], s * d)
        return chip_at(s * d, 0)

    def ends(name, me):
        kind = name[0]
        if kind == "SU":
            at = pl.ds(zat[name[1]], 1)
            return store.at[0, :, at], store.at[1, :, at]
        if kind in ("SWI", "SWO"):
            dst = weights(kind[1:], name[1], (0, 2), me)
            return ((wi if kind == "SWI" else wo) if name[1] == 0 else dst), dst
        if kind in ("WI", "WO"):
            s, d = name[1:]
            slots = (0, 2) if d < 4 else ((0, 1) if s > 0 else (1, 1))
            dst = weights(kind, -s * (d - me), slots, 1)
            if d > 1:
                return dst, dst
            return (wi if kind == "WI" else wo), dst
        if kind in ("UX", "VX"):
            _, s, d, h = name
            half = hop_x[(kind[0], s)]
            first, count = (0, NZ) if d == 1 else ((0, 4) if s > 0 else (4, 4))
            if h == 1:
                frm = pool.at[pl.ds(chips_row[(s * d) % NX] + first, count)]
                if d == 2:
                    return frm, hop.at[pl.ds(4 * half, 4)]
            else:
                frm = hop.at[pl.ds(4 * half, 4)]
            return frm, xb.at[xat[-s * (h - me) % NX], pl.ds(first, count)]
        if kind in ("UZ", "VZ"):
            _, s, d, h = name
            first, count = (0, 4) if d < 4 else ((0, 2) if s > 0 else (2, 2))
            if h == 1:
                frm = xb.at[pl.ds(first, count), pl.ds(zat[s * d % NZ], 1)]
            else:
                frm = zt.at[pl.ds(transit[(kind, s, d, h - 1)], count)]
            if h < d:
                return frm, zt.at[pl.ds(transit[name], count)]
            began = pl.ds(zat[-s * (h - me) % NZ], 1)
            if kind == "UZ":
                return frm, store.at[0, pl.ds(first, count), began]
            raise ValueError(kind)
        lo, hi = span[name]
        if kind in ("A", "B", "C", "D", "E"):
            return part.at[block(name, 0), pl.ds(lo, hi - lo)], land.at[pl.ds(base[name], hi - lo)]
        s, d = name[-2:]
        off = -s * (d - me)
        dx, dz = {"PZ": (0, off), "QX": (off, 0), "PX": (off, name[1]), "QZ": (name[1], off)}[kind]
        dst = g.at[chip_at(dx, dz), pl.ds(lo, hi - lo)]
        mine = me == 1 and dx % NX == 0 and dz % NZ == 0
        return (xt.at[pl.ds(lo, hi - lo)] if mine else dst), dst

    def remote(name, me):
        src, dst = ends(name, me)
        i = index[name]
        return pltpu.make_async_remote_copy(
            src_ref=src if me else dst,
            dst_ref=dst,
            send_sem=ssem.at[i],
            recv_sem=rsem.at[i],
            device_id=peer[items[name][0]],
            device_id_type=MESH,
        )

    def fold(name):
        lo, hi = span[name]
        b = block(name, 1)

        def body(i, _):
            to = pl.ds(pl.multiple_of(lo + i * 16, 16), 16)
            src = pl.ds(pl.multiple_of(base[name] + i * 16, 16), 16)
            part[b, to, :] = (
                part[b, to, :].astype(jnp.float32) + land[src, :].astype(jnp.float32)
            ).astype(jnp.bfloat16)
            return 0

        lax.fori_loop(0, (hi - lo) // 16, body, 0)

    def keep(tag):
        at = pl.ds(zat[0], 1)
        item = pltpu.make_async_copy(xb.at[:, at], store.at[0, :, at], lsem.at[4])
        item.start()
        item.wait()

    for op, name in order:
        if op == "wait":
            remote(name, 0).wait_recv()
        elif items[name][0][0] != "t":
            remote(name, 1).start()
        elif name[0] == "fold":
            fold(name[1])
        else:
            for item in pending.pop(name):
                item.wait()
            if name[0] == "own":
                keep(name[1])
    for item in pending.pop("last", []):
        item.wait()
    if stage:
        out[...] = part[own]
    for name in copies:
        remote(name, 1).wait_send()


PAIR = (2, PIECE, 128)


def semaphores(stage):
    count = sum(1 for item in plan(stage)[0].values() if item[0][0] != "t")
    return [
        pltpu.SemaphoreType.DMA((count,)),
        pltpu.SemaphoreType.DMA((count,)),
        pltpu.SemaphoreType.DMA((CHIPS,)),
    ]


def params_of(stage):
    return pltpu.CompilerParams(
        collective_id=stage, has_side_effects=True, vmem_limit_bytes=VMEM_LIMIT
    )


COST = pl.CostEstimate(flops=0, bytes_accessed=200_000_000, transcendentals=0)
SHAPES = ((CHIPS, ROWS, D), (4, D, 2 * H), (4, H, D))


def gather(xt, wi, wo, pool):
    vmem, anywhere = pl.BlockSpec(memory_space=pltpu.VMEM), pl.BlockSpec(memory_space=pl.ANY)
    return pl.pallas_call(
        gather_kernel,
        out_shape=[jax.ShapeDtypeStruct(n, jnp.bfloat16) for n in SHAPES + ((2, NX, NZ) + PAIR,)],
        in_specs=[vmem, vmem, vmem, anywhere],
        out_specs=[anywhere] * 4,
        scratch_shapes=[
            pltpu.VMEM((NX, NZ) + PAIR, jnp.bfloat16),
            pltpu.VMEM((36, 1) + PAIR, jnp.bfloat16),
            pltpu.VMEM((8,) + PAIR, jnp.bfloat16),
        ]
        + semaphores(0),
        compiler_params=params_of(0),
        cost_estimate=COST,
        name="gather",
    )(xt, wi, wo, pool)


def reduce(part):
    span = plan(1)[1]
    landing = sum(hi - lo for name, (lo, hi) in span.items() if name[0] in ("A", "B", "C", "D", "E"))
    return pl.pallas_call(
        reduce_kernel,
        out_shape=jax.ShapeDtypeStruct((TOK, D), jnp.bfloat16),
        in_specs=[pl.BlockSpec(memory_space=pl.ANY)],
        out_specs=pl.BlockSpec(memory_space=pltpu.VMEM),
        scratch_shapes=[
            pltpu.VMEM((CHIPS, TOK, D), jnp.bfloat16),
            pltpu.VMEM((landing, D), jnp.bfloat16),
        ]
        + semaphores(1),
        compiler_params=params_of(1),
        cost_estimate=COST,
        name="reduce",
    )(part)


STEP = 8


def expert_kernel(es, g, wi, wo, part, gv, wiv, wov, xs, ys, cnt, wgt, rank, sel, outv, isem, wsem, osem):
    nchunk = CHIPS // STEP
    for n in range(nchunk):
        pltpu.make_async_copy(g.at[pl.ds(n * STEP, STEP)], gv.at[pl.ds(n * STEP, STEP)], isem.at[n]).start()
    for j in range(4):
        pltpu.make_async_copy(wi.at[j], wiv.at[j], wsem.at[j]).start()
        pltpu.make_async_copy(wo.at[j], wov.at[j], wsem.at[4 + j]).start()
    tri = (
        lax.broadcasted_iota(jnp.int32, (TOK, TOK), 0) <= lax.broadcasted_iota(jnp.int32, (TOK, TOK), 1)
    ).astype(jnp.bfloat16)
    line = lax.broadcasted_iota(jnp.int32, (CAP, TOK), 0).astype(jnp.float32)
    experts = [es[j].astype(jnp.float32) for j in range(4)]
    for n in range(nchunk):
        pltpu.make_async_copy(
            g.at[pl.ds(n * STEP, STEP)], gv.at[pl.ds(n * STEP, STEP)], isem.at[n]
        ).wait()

        def count(i, _):
            b = n * STEP + i
            meta = gv[b, TOK:ROWS, 0 : 3 * TOK].astype(jnp.float32)
            ids, share = meta[:, 0:TOK], meta[:, TOK : 2 * TOK] + meta[:, 2 * TOK :]
            named = [ids == experts[j] for j in range(4)]
            ones = [jnp.sum(jnp.where(m, 1.0, 0.0), axis=0, keepdims=True) for m in named]
            held = [jnp.sum(jnp.where(m, share, 0.0), axis=0, keepdims=True) for m in named]
            rows = pl.ds(pl.multiple_of(b * 8, 8), 8)
            cnt[rows, :] = jnp.concatenate(ones + ones, axis=0)
            wgt[rows, :] = jnp.concatenate(held + held, axis=0)
            return 0

        lax.fori_loop(0, STEP, count, 0)
        rows = pl.ds(n * STEP * 8, STEP * 8)
        chosen = cnt[rows, :]
        upto = jnp.dot(chosen.astype(jnp.bfloat16), tri, preferred_element_type=jnp.float32)
        rank[rows, :] = jnp.where(chosen > 0.5, upto - 1.0, -1.0)

        def pick(i, _):
            b = n * STEP + i
            rows = pl.ds(pl.multiple_of(b * 8, 8), 8)
            place8, held8 = rank[rows, :], wgt[rows, :]
            hit = [line == place8[j : j + 1, :] for j in range(4)]
            onehot = jnp.concatenate([jnp.where(m, 1.0, 0.0) for m in hit], axis=0)
            weight = jnp.concatenate(
                [jnp.where(hit[j], held8[j : j + 1, :], 0.0) for j in range(4)], axis=0
            )
            high = weight.astype(jnp.bfloat16)
            sel[b, 0 : 4 * CAP, :] = high
            sel[b, 4 * CAP :, :] = (weight - high.astype(jnp.float32)).astype(jnp.bfloat16)
            got = jnp.dot(
                onehot.astype(jnp.bfloat16), gv[b, 0:TOK, :], preferred_element_type=jnp.float32
            ).astype(jnp.bfloat16)
            at = pl.ds(pl.multiple_of(b * CAP, CAP), CAP)
            for j in range(4):
                xs[j, at, :] = got[j * CAP : (j + 1) * CAP, :]
            return 0

        lax.fori_loop(0, STEP, pick, 0, unroll=2)
    for j in range(4):
        pltpu.make_async_copy(wi.at[j], wiv.at[j], wsem.at[j]).wait()
        pltpu.make_async_copy(wo.at[j], wov.at[j], wsem.at[4 + j]).wait()

    def mlp(i, _):
        j, at = i // 2, pl.ds(pl.multiple_of(lax.rem(i, 2) * 256, 256), 256)
        both = jnp.dot(xs[j, at, :], wiv[j], preferred_element_type=jnp.float32)
        hidden = (jax.nn.silu(both[:, :H]) * both[:, H:]).astype(jnp.bfloat16)
        ys[j, at, :] = jnp.dot(hidden, wov[j], preferred_element_type=jnp.float32).astype(jnp.bfloat16)
        return 0

    lax.fori_loop(0, 8, mlp, 0)
    for n in range(nchunk):

        def spread(i, _):
            b = n * STEP + i
            at = pl.ds(pl.multiple_of(b * CAP, CAP), CAP)
            rows = jnp.concatenate([ys[j, at, :] for j in range(4)] * 2, axis=0)
            outv[b] = lax.dot_general(
                sel[b], rows, (((0,), (0,)), ((), ())), preferred_element_type=jnp.float32
            ).astype(jnp.bfloat16)
            return 0

        lax.fori_loop(0, STEP, spread, 0, unroll=2)
        pltpu.make_async_copy(outv.at[pl.ds(n * STEP, STEP)], part.at[pl.ds(n * STEP, STEP)], osem.at[n]).start()
    for n in range(nchunk):
        pltpu.make_async_copy(
            outv.at[pl.ds(n * STEP, STEP)], part.at[pl.ds(n * STEP, STEP)], osem.at[n]
        ).wait()


def experts_of(es, g, wi, wo):
    any_space = pl.BlockSpec(memory_space=pl.ANY)
    nchunk = CHIPS // STEP
    return pl.pallas_call(
        expert_kernel,
        out_shape=jax.ShapeDtypeStruct((CHIPS, TOK, D), jnp.bfloat16),
        in_specs=[pl.BlockSpec(memory_space=pltpu.SMEM)] + [any_space] * 3,
        out_specs=any_space,
        scratch_shapes=[
            pltpu.VMEM((CHIPS, ROWS, D), jnp.bfloat16),
            pltpu.VMEM((4, D, 2 * H), jnp.bfloat16),
            pltpu.VMEM((4, H, D), jnp.bfloat16),
            pltpu.VMEM((4, CHIPS * CAP, D), jnp.bfloat16),
            pltpu.VMEM((4, CHIPS * CAP, D), jnp.bfloat16),
            pltpu.VMEM((CHIPS * 8, TOK), jnp.float32),
            pltpu.VMEM((CHIPS * 8, TOK), jnp.float32),
            pltpu.VMEM((CHIPS * 8, TOK), jnp.float32),
            pltpu.VMEM((CHIPS, 8 * CAP, TOK), jnp.bfloat16),
            pltpu.VMEM((CHIPS, TOK, D), jnp.bfloat16),
            pltpu.SemaphoreType.DMA((nchunk,)),
            pltpu.SemaphoreType.DMA((8,)),
            pltpu.SemaphoreType.DMA((nchunk,)),
        ],
        compiler_params=pltpu.CompilerParams(vmem_limit_bytes=VMEM_LIMIT),
        cost_estimate=pl.CostEstimate(flops=6_000_000_000, bytes_accessed=40_000_000, transcendentals=0),
        name="experts",
    )(es, g, wi, wo)


def tiles_of(array):
    slots, columns = array.shape[0], array.shape[-1]
    rows = array.size // slots // columns
    tiled = array.reshape(slots, rows // 8, 8, columns // 128, 128)
    return tiled.transpose(0, 1, 3, 2, 4).reshape(slots, -1, 8, 128)


def untile(tiles, shape):
    slots, columns = shape[0], shape[-1]
    tiled = tiles.reshape(slots, -1, columns // 128, 8, 128)
    return tiled.transpose(0, 1, 3, 2, 4).reshape(shape)


def on_device(
    tokens, w_in, w_out, moments_in, moments_out, expert_ids, route_weights, old_plan, new_plan
):
    devices = lax.axis_size("exp")
    slots = 2 * devices
    slot_index = jnp.arange(slots, dtype=jnp.int32)
    same_expert = new_plan[:, None] == old_plan[None, :]
    source = jnp.min(jnp.where(same_expert, slot_index[None, :], slots), axis=1)

    state = [w_in, w_out, moments_in, moments_out]
    pooled = jnp.concatenate(
        [tiles_of(a) for a in state]
        + [jnp.zeros((2, CHIPS * CHUNK - TILES, 8, 128), jnp.bfloat16)],
        axis=1,
    )
    pooled = pooled.reshape(2, CHIPS, PIECE, 128).transpose(1, 0, 2, 3)

    share = route_weights / jnp.sum(route_weights, axis=1, keepdims=True)
    meta = jnp.concatenate(
        [
            expert_ids.T.astype(jnp.bfloat16),
            share.T.astype(jnp.bfloat16),
            (share.T - lax.reduce_precision(share.T, 8, 7)).astype(jnp.bfloat16),
            jnp.zeros((META, D - 3 * TOK), jnp.bfloat16),
        ],
        axis=1,
    )
    earlier = (old_plan[:, None] == old_plan[None, :]) & (slot_index[None, :] < slot_index[:, None])
    computes = jnp.where(jnp.any(earlier, axis=1), -1, old_plan)
    es = lax.dynamic_slice(computes, (lax.axis_index("exp") // 2 * 4,), (4,))
    sent = jnp.concatenate([tokens, meta], axis=0)
    g, gi, go, store = gather(sent, w_in, w_out, pooled)
    core = lax.axis_index("exp") % 2
    row = (source // 2 % 2 != core) * (2 * CHIPS) + source // 4 * 2 + source % 2
    picked = jnp.take(store.reshape(8 * CHIPS, PIECE // 2, 128), 2 * row + core, axis=0, mode="clip")
    picked, g = lax.optimization_barrier((picked, g))
    landed = lax.all_to_all(
        picked.reshape(devices, 2, PIECE // 2, 128), "exp", split_axis=0, concat_axis=0, tiled=True
    )
    mixed = reduce(experts_of(es, g, gi, go))
    tiles = landed.transpose(1, 0, 2, 3)
    tiles = tiles.reshape(2, CHIPS * CHUNK, 8, 128)
    outs, at = [], 0
    for a in state:
        count = a.size // 2 // 1024
        outs.append(untile(tiles[:, at : at + count], a.shape))
        at += count
    return (mixed, *outs)


def solution(mesh):
    return jax.shard_map(
        on_device,
        mesh=mesh,
        in_specs=(
            P(("grp", "exp"), None),
            P("exp", "grp", None),
            P("exp", "grp", None),
            P("exp", None, "grp", None),
            P("exp", None, "grp", None),
            P(("grp", "exp"), None),
            P(("grp", "exp"), None),
            P(),
            P(),
        ),
        out_specs=(
            P(("grp", "exp"), None),
            P("exp", "grp", None),
            P("exp", "grp", None),
            P("exp", None, "grp", None),
            P("exp", None, "grp", None),
        ),
        check_vma=False,
    )
```

```python
import functools
import heapq

import jax
import jax.numpy as jnp
from jax import lax
from jax.experimental import pallas as pl
from jax.experimental.pallas import tpu as pltpu
from jax.sharding import PartitionSpec as P

TOP = 8
TOK = 128
D = 1024
H = 384
NX, NZ, NY = 4, 8, 8
META = 8
ROWS = TOK + META
CAP = 16
CHIPS = NX * NZ
MESH = pl.DeviceIdType.MESH
VMEM_LIMIT = 63 * 1024 * 1024
TILES = 432
CHUNK = 14
PIECE = CHUNK * 8
GATHER_ROWS = 104
REDUCE_ROWS = 80
AHEAD = 4000.0
BESIDE = 25000.0
RATE = 43.3
HOP = 1500.0
GROUPS = (0, 1, 7, 2, 6, 3, 5, 4)
SPREAD = (4, 3, 5, 2, 6, 1, 7, 0)
TORUS = (("x", 1), ("x", -1), ("z", 1), ("z", -1))
LINKS = TORUS + (("y", 1), ("y", -1), ("c", 0))


def order_of(items, beside=0.0):
    after, missing, tail = {n: [] for n in items}, {}, {}
    for name, (_, _, deps) in items.items():
        missing[name] = len(set(deps))
        for d in set(deps):
            after[d].append(name)

    def lag(name):
        axis = items[name][0][0]
        return 0.0 if axis == "t" else 500.0 if axis == "c" else HOP

    def measure(name):
        if name not in tail:
            later = max([measure(n) for n in after[name]], default=0.0)
            tail[name] = items[name][1] + lag(name) + later
        return tail[name]

    place_of = {name: i for i, name in enumerate(items)}
    ready = {item[0][:2]: [] for item in items.values()}
    free, heap, ops, busy = dict.fromkeys(ready, 0.0), [], [], [False]

    def push(name):
        heapq.heappush(ready[items[name][0][:2]], (-measure(name), place_of[name], name))

    def issue(now):
        for link, queue in ready.items():
            while queue and (not busy[0] if link[0] == "t" else free[link] - now < AHEAD):
                name = heapq.heappop(queue)[2]
                busy[0] = busy[0] or link[0] == "t"
                begin = max(now, free[link])
                slow = {"z": 2.0, "x": 1.5}.get(link[0], 1.0) if begin < beside else 1.0
                free[link] = begin + slow * items[name][1]
                heapq.heappush(heap, (free[link] + lag(name), len(ops), name))
                ops.append(("start", name))

    for name in items:
        if not missing[name]:
            push(name)
    now = 0.0
    issue(now)
    while heap:
        now, _, name = heapq.heappop(heap)
        if items[name][0][0] == "t":
            busy[0] = False
        else:
            ops.append(("wait", name))
        for later in after[name]:
            missing[later] -= 1
            if not missing[later]:
                push(later)
        issue(now)
    return ops, now


def split(lo, hi, s, unit=8):
    mid = lo + -(-(hi - lo) // (2 * unit)) * unit
    return (lo, mid) if s > 0 else (mid, hi)


def ring(kind, at):
    size = NX if kind[0][1] == "X" else NZ
    at, half = at % size, size // 2
    if at == 0:
        return []
    if at == half:
        return [kind + (1, half), kind + (-1, half)]
    return [kind + (-1, at)] if at < half else [kind + (1, size - at)]


def plan(stage):
    items, span = {}, {}

    def copy(name, link, count, deps):
        items[name] = (link, count / (600.0 if link[0] == "c" else RATE), deps)

    def rows(name, link, lo, hi, deps):
        span[name] = (lo, hi)
        copy(name, link, (hi - lo) * D * 2, deps)

    def step(name, time, deps):
        items[name] = (("t", 0), time, deps)

    pr = GATHER_ROWS
    for s in (1, -1):
        for d in (1, 2, 3, 4):
            lo, hi = split(0, pr, s) if d == 4 else (0, pr)
            rows(("PZ", s, d), ("z", s), lo, hi, [("PZ", s, d - 1)] if d > 1 else [])
        for d in (1, 2):
            lo, hi = split(pr, ROWS, s) if d == 2 else (pr, ROWS)
            rows(("QX", s, d), ("x", s), lo, hi, [("QX", s, 1)] if d > 1 else [])
    for s in (1, -1):
        for d in (1, 2, 3, 4):
            for kind, count in (("WI", 393216), ("WO", 196608)):
                deps = [(kind, s, d - 1)] if d > 1 else []
                copy((kind, s, d), ("y", s), count // (2 if d == 4 else 1), deps)
    for dz in GROUPS:
        for s in (1, -1):
            rows(("PX", dz, s, 1), ("x", s), 0, pr, ring(("PZ",), dz))
            rows(("PX", dz, s, 2), ("x", s), *split(0, pr, s), [("PX", dz, s, 1)])
    for dx in (0, 1, 3, 2):
        for s in (1, -1):
            for d in (1, 2, 3, 4):
                lo, hi = split(pr, ROWS, s) if d == 4 else (pr, ROWS)
                deps = [("QZ", dx, s, d - 1)] if d > 1 else ring(("QX",), dx)
                rows(("QZ", dx, s, d), ("z", s), lo, hi, deps)
    weights = []
    for dy in range(NY):
        for kind, count in (("WI", 393216), ("WO", 196608)):
            copy(("S" + kind, dy), ("c", 0), count, ring((kind + "Y",), dy) and [
                (kind,) + k[1:] for k in ring((kind + "Y",), dy)
            ])
            weights += [("S" + kind, dy)] + items[("S" + kind, dy)][2]

    piece = 2 * PIECE * 128 * 2

    def exchange(tag, after):
        for s in (1, -1):
            copy((tag + "X", s, 2, 1), ("x", s), 4 * piece, after)
            copy((tag + "X", s, 1, 1), ("x", s), 8 * piece, after)
            copy((tag + "X", s, 2, 2), ("x", s), 4 * piece, [(tag + "X", s, 2, 1)])
        ends = [(tag + "X", s, d, d) for s in (1, -1) for d in (1, 2)]
        step(("own", tag), 800.0, ends + after)
        for h in (1, 2, 3, 4):
            for d in (4, 3, 2, 1):
                for s in (1, -1):
                    if d >= h:
                        deps = [(tag + "Z", s, d, h - 1)] if h > 1 else [("own", tag)]
                        copy((tag + "Z", s, d, h), ("z", s), (2 if d == 4 else 4) * piece, deps)
        return [(tag + "Z", s, d, d) for s in (1, -1) for d in (1, 2, 3, 4)]

    ends = exchange("U", [])
    for dz in range(NZ):
        deps = [k + (k[2],) for k in ring(("UZ",), dz)]
        copy(("SU", dz), ("c", 0), 4 * piece, deps or [("own", "U")])

    for dz in SPREAD:
        step(("sum", dz), 300.0, [])

    pr = REDUCE_ROWS

    def fold(name, dz):
        step(("fold", name), 60.0 + 3.0 * (span[name][1] - span[name][0]), [name, ("sum", dz % NZ)])

    for dz in SPREAD:
        for s in (1, -1):
            rows(("A", dz, s), ("x", s), *split(0, pr, s, 16), [("sum", dz)])
            fold(("A", dz, s), dz)
        if dz == 4:
            for dx in (2, 1, 3, 0):
                for s in (1, -1):
                    rows(("D", dx, s, 4), ("z", s), *split(pr, TOK, s, 16), [("sum", 4)])
                    fold(("D", dx, s, 4), 3 * s)
    for dx in (2, 1, 3, 0):
        for s in (1, -1):
            for d in (3, 2, 1):
                deps = [("fold", ("D", dx, s, d + 1)), ("sum", (s * d) % NZ)]
                rows(("D", dx, s, d), ("z", s), pr, TOK, deps)
                fold(("D", dx, s, d), s * (d - 1))
    for s in (1, -1):
        for d in (2, 1):
            dx = (s * d) % NX
            deps = [("fold", ("D", dx, 1, 1)), ("fold", ("D", dx, -1, 1))]
            deps += [("fold", ("E", s, 2))] if d < 2 else []
            rows(("E", s, d), ("x", s), *(split(pr, TOK, s, 16) if d == 2 else (pr, TOK)), deps)
            fold(("E", s, d), 0)
    for dz in SPREAD:
        for s in (1, -1):
            rows(("B", dz, s), ("x", s), 0, pr, [("fold", ("A", dz, s)), ("sum", dz)])
            fold(("B", dz, s), dz)
    for s in (1, -1):
        for d in (4, 3, 2, 1):
            dz = (s * d) % NZ
            deps = [("fold", ("B", dz, 1)), ("fold", ("B", dz, -1))]
            deps += [("fold", ("C", s, d + 1))] if d < 4 else []
            rows(("C", s, d), ("z", s), *(split(0, pr, s, 16) if d == 4 else (0, pr)), deps)
            fold(("C", s, d), s * (d - 1))
    first = {
        name: item for name, item in items.items()
        if name[0][0] in "PQWSU" or name == ("own", "U")
    }
    first = {n: (link, t, [d for d in deps if d in first]) for n, (link, t, deps) in first.items()}
    rest = {n: item for n, item in items.items() if n not in first}
    rest = {n: (link, t, [d for d in deps if d in rest]) for n, (link, t, deps) in rest.items()}
    return first if stage == 0 else rest, span


def gather_kernel(xt, wi, wo, pool, g, gi, go, store, xb, zt, hop, ssem, rsem, lsem):
    run(0, xt, wi, wo, pool, None, g, gi, go, None, None, store, xb, zt, hop, ssem, rsem, lsem, None)


def reduce_kernel(psrc, out, part, land, ssem, rsem, lsem):
    run(1, None, None, None, None, out, None, None, None, part, land, None, None, None, None,
        ssem, rsem, lsem, psrc)


def run(
    stage, xt, wi, wo, pool, out, g, gi, go, part, land, store, xb, zt, hop, ssem, rsem, lsem, psrc,
):
    y = lax.axis_index("grp")
    e = lax.axis_index("exp")
    c = lax.rem(e, 2)
    x, z = e // (2 * NZ), lax.rem(e // 2, NZ)
    xat = [x] + [lax.rem(x + d, NX) for d in range(1, NX)]
    zat = [z] + [lax.rem(z + d, NZ) for d in range(1, NZ)]
    yat = [y] + [lax.rem(y + d, NY) for d in range(1, NY)]
    chips = [[xat[dx] * NZ + zat[dz] for dz in range(NZ)] for dx in range(NX)]
    peer = {("c", 0): (y, e + 1 - 2 * c)}
    for s in (1, -1):
        peer[("x", s)] = (y, 2 * chips[s % NX][0] + c)
        peer[("z", s)] = (y, 2 * chips[0][s % NZ] + c)
        peer[("y", s)] = (yat[s % NY], e)
    span_at = {
        "I": [pl.multiple_of(yat[d] * 128, 128) for d in range(NY)],
        "O": [pl.multiple_of(yat[d] * 48, 16) for d in range(NY)],
    }
    other = 1 - c
    chips_row = [xat[dx] * NZ for dx in range(NX)]
    first_slot = [2 * c, 2 * c + 1, 2 * (1 - c)]

    def chip_at(dx, dz):
        return chips[dx % NX][dz % NZ]

    items, span = plan(stage)
    order, _ = order_of(items, BESIDE if stage else 0.0)
    copies = [name for name, item in items.items() if item[0][0] != "t"]
    index = {name: i for i, name in enumerate(copies)}
    base, top = {}, 0
    for name in copies:
        if name[0] in ("A", "B", "C", "D", "E"):
            base[name] = top
            top += span[name][1] - span[name][0]
    transit, top = {}, {"U": 0, "V": 0}
    for name in copies:
        if name[0] in ("UZ", "VZ") and name[2] != name[3]:
            transit[name] = top[name[0][0]]
            top[name[0][0]] += 2 if name[2] == 4 else 4
    hop_x = {("U", 1): 0, ("U", -1): 1, ("V", 1): 0, ("V", -1): 1}

    own = chip_at(0, 0)
    def weights(kind, dy, slots, mine):
        ref, size = (gi, 128) if kind == "WI" else (go, 48)
        first = first_slot[slots[0]] if mine else first_slot[2]
        return ref.at[pl.ds(first, slots[1]), pl.ds(span_at[kind[1]][dy % NY], size)]

    links = LINKS if stage == 0 else TORUS
    pending = {}
    if stage == 0:
        pending["last"] = [
            pltpu.make_async_copy(xt, g.at[own], lsem.at[0]),
            pltpu.make_async_copy(wi, weights("WI", 0, (0, 2), 1), lsem.at[1]),
            pltpu.make_async_copy(wo, weights("WO", 0, (0, 2), 1), lsem.at[2]),
        ]
        pending["own", "U"] = [pltpu.make_async_copy(pool.at[pl.ds(chips_row[0], NZ)], xb.at[x], lsem.at[3])]
    else:
        for n, dz in enumerate(SPREAD):
            pending["sum", dz] = [
                pltpu.make_async_copy(psrc.at[chip_at(dx, dz)], part.at[chip_at(dx, dz)], lsem.at[NX * n + dx])
                for dx in range(NX)
            ]
    for group in pending.values():
        for item in group:
            item.start()
    barrier = pltpu.get_barrier_semaphore()
    for link in links:
        pl.semaphore_signal(barrier, inc=1, device_id=peer[link], device_id_type=MESH)
    pl.semaphore_wait(barrier, len(links))

    def block(name, shift):
        kind, s = name[0], name[2] if name[0] in "ABD" else name[1]
        if kind == "A":
            return chip_at(s * (2 - shift), name[1])
        if kind == "B":
            return chip_at(s * (1 - shift), name[1])
        d = name[-1] - shift
        if kind == "C":
            return chip_at(0, s * d)
        if kind == "D":
            return chip_at(name[1], s * d)
        return chip_at(s * d, 0)

    def ends(name, me):
        kind = name[0]
        if kind == "SU":
            at = pl.ds(zat[name[1]], 1)
            return store.at[0, :, at], store.at[1, :, at]
        if kind in ("SWI", "SWO"):
            dst = weights(kind[1:], name[1], (0, 2), me)
            return ((wi if kind == "SWI" else wo) if name[1] == 0 else dst), dst
        if kind in ("WI", "WO"):
            s, d = name[1:]
            slots = (0, 2) if d < 4 else ((0, 1) if s > 0 else (1, 1))
            dst = weights(kind, -s * (d - me), slots, 1)
            if d > 1:
                return dst, dst
            return (wi if kind == "WI" else wo), dst
        if kind in ("UX", "VX"):
            _, s, d, h = name
            half = hop_x[(kind[0], s)]
            first, count = (0, NZ) if d == 1 else ((0, 4) if s > 0 else (4, 4))
            if h == 1:
                frm = pool.at[pl.ds(chips_row[(s * d) % NX] + first, count)]
                if d == 2:
                    return frm, hop.at[pl.ds(4 * half, 4)]
            else:
                frm = hop.at[pl.ds(4 * half, 4)]
            return frm, xb.at[xat[-s * (h - me) % NX], pl.ds(first, count)]
        if kind in ("UZ", "VZ"):
            _, s, d, h = name
            first, count = (0, 4) if d < 4 else ((0, 2) if s > 0 else (2, 2))
            if h == 1:
                frm = xb.at[pl.ds(first, count), pl.ds(zat[s * d % NZ], 1)]
            else:
                frm = zt.at[pl.ds(transit[(kind, s, d, h - 1)], count)]
            if h < d:
                return frm, zt.at[pl.ds(transit[name], count)]
            began = pl.ds(zat[-s * (h - me) % NZ], 1)
            if kind == "UZ":
                return frm, store.at[0, pl.ds(first, count), began]
            raise ValueError(kind)
        lo, hi = span[name]
        if kind in ("A", "B", "C", "D", "E"):
            return part.at[block(name, 0), pl.ds(lo, hi - lo)], land.at[pl.ds(base[name], hi - lo)]
        s, d = name[-2:]
        off = -s * (d - me)
        dx, dz = {"PZ": (0, off), "QX": (off, 0), "PX": (off, name[1]), "QZ": (name[1], off)}[kind]
        dst = g.at[chip_at(dx, dz), pl.ds(lo, hi - lo)]
        mine = me == 1 and dx % NX == 0 and dz % NZ == 0
        return (xt.at[pl.ds(lo, hi - lo)] if mine else dst), dst

    def remote(name, me):
        src, dst = ends(name, me)
        i = index[name]
        return pltpu.make_async_remote_copy(
            src_ref=src if me else dst,
            dst_ref=dst,
            send_sem=ssem.at[i],
            recv_sem=rsem.at[i],
            device_id=peer[items[name][0]],
            device_id_type=MESH,
        )

    def fold(name):
        lo, hi = span[name]
        b = block(name, 1)

        def body(i, _):
            to = pl.ds(pl.multiple_of(lo + i * 16, 16), 16)
            src = pl.ds(pl.multiple_of(base[name] + i * 16, 16), 16)
            part[b, to, :] = (
                part[b, to, :].astype(jnp.float32) + land[src, :].astype(jnp.float32)
            ).astype(jnp.bfloat16)
            return 0

        lax.fori_loop(0, (hi - lo) // 16, body, 0)

    def keep(tag):
        at = pl.ds(zat[0], 1)
        item = pltpu.make_async_copy(xb.at[:, at], store.at[0, :, at], lsem.at[4])
        item.start()
        item.wait()

    for op, name in order:
        if op == "wait":
            remote(name, 0).wait_recv()
        elif items[name][0][0] != "t":
            remote(name, 1).start()
        elif name[0] == "fold":
            fold(name[1])
        else:
            for item in pending.pop(name):
                item.wait()
            if name[0] == "own":
                keep(name[1])
    for item in pending.pop("last", []):
        item.wait()
    if stage:
        out[...] = part[own]
    for name in copies:
        remote(name, 1).wait_send()


PAIR = (2, PIECE, 128)


def semaphores(stage):
    count = sum(1 for item in plan(stage)[0].values() if item[0][0] != "t")
    return [
        pltpu.SemaphoreType.DMA((count,)),
        pltpu.SemaphoreType.DMA((count,)),
        pltpu.SemaphoreType.DMA((CHIPS,)),
    ]


def params_of(stage):
    return pltpu.CompilerParams(
        collective_id=stage, has_side_effects=True, vmem_limit_bytes=VMEM_LIMIT
    )


COST = pl.CostEstimate(flops=0, bytes_accessed=200_000_000, transcendentals=0)
SHAPES = ((CHIPS, ROWS, D), (4, D, 2 * H), (4, H, D))


def gather(xt, wi, wo, pool):
    vmem, anywhere = pl.BlockSpec(memory_space=pltpu.VMEM), pl.BlockSpec(memory_space=pl.ANY)
    return pl.pallas_call(
        gather_kernel,
        out_shape=[jax.ShapeDtypeStruct(n, jnp.bfloat16) for n in SHAPES + ((2, NX, NZ) + PAIR,)],
        in_specs=[vmem, vmem, vmem, anywhere],
        out_specs=[anywhere] * 4,
        scratch_shapes=[
            pltpu.VMEM((NX, NZ) + PAIR, jnp.bfloat16),
            pltpu.VMEM((36, 1) + PAIR, jnp.bfloat16),
            pltpu.VMEM((8,) + PAIR, jnp.bfloat16),
        ]
        + semaphores(0),
        compiler_params=params_of(0),
        cost_estimate=COST,
        name="gather",
    )(xt, wi, wo, pool)


def reduce(part):
    span = plan(1)[1]
    landing = sum(hi - lo for name, (lo, hi) in span.items() if name[0] in ("A", "B", "C", "D", "E"))
    return pl.pallas_call(
        reduce_kernel,
        out_shape=jax.ShapeDtypeStruct((TOK, D), jnp.bfloat16),
        in_specs=[pl.BlockSpec(memory_space=pl.ANY)],
        out_specs=pl.BlockSpec(memory_space=pltpu.VMEM),
        scratch_shapes=[
            pltpu.VMEM((CHIPS, TOK, D), jnp.bfloat16),
            pltpu.VMEM((landing, D), jnp.bfloat16),
        ]
        + semaphores(1),
        compiler_params=params_of(1),
        cost_estimate=COST,
        name="reduce",
    )(part)


STEP = 8


def expert_kernel(es, g, wi, wo, part, gv, wiv, wov, xs, ys, cnt, wgt, rank, sel, outv, isem, wsem, osem):
    nchunk = CHIPS // STEP
    for n in range(nchunk):
        pltpu.make_async_copy(g.at[pl.ds(n * STEP, STEP)], gv.at[pl.ds(n * STEP, STEP)], isem.at[n]).start()
    for j in range(4):
        pltpu.make_async_copy(wi.at[j], wiv.at[j], wsem.at[j]).start()
        pltpu.make_async_copy(wo.at[j], wov.at[j], wsem.at[4 + j]).start()
    tri = (
        lax.broadcasted_iota(jnp.int32, (TOK, TOK), 0) <= lax.broadcasted_iota(jnp.int32, (TOK, TOK), 1)
    ).astype(jnp.bfloat16)
    line = lax.broadcasted_iota(jnp.int32, (CAP, TOK), 0).astype(jnp.float32)
    experts = [es[j].astype(jnp.float32) for j in range(4)]
    for n in range(nchunk):
        pltpu.make_async_copy(
            g.at[pl.ds(n * STEP, STEP)], gv.at[pl.ds(n * STEP, STEP)], isem.at[n]
        ).wait()

        def count(i, _):
            b = n * STEP + i
            meta = gv[b, TOK:ROWS, 0 : 3 * TOK].astype(jnp.float32)
            ids, share = meta[:, 0:TOK], meta[:, TOK : 2 * TOK] + meta[:, 2 * TOK :]
            named = [ids == experts[j] for j in range(4)]
            ones = [jnp.sum(jnp.where(m, 1.0, 0.0), axis=0, keepdims=True) for m in named]
            held = [jnp.sum(jnp.where(m, share, 0.0), axis=0, keepdims=True) for m in named]
            rows = pl.ds(pl.multiple_of(b * 8, 8), 8)
            cnt[rows, :] = jnp.concatenate(ones + ones, axis=0)
            wgt[rows, :] = jnp.concatenate(held + held, axis=0)
            return 0

        lax.fori_loop(0, STEP, count, 0, unroll=4)
        rows = pl.ds(n * STEP * 8, STEP * 8)
        chosen = cnt[rows, :]
        upto = jnp.dot(chosen.astype(jnp.bfloat16), tri, preferred_element_type=jnp.float32)
        rank[rows, :] = jnp.where(chosen > 0.5, upto - 1.0, -1.0)

        def pick(i, _):
            b = n * STEP + i
            rows = pl.ds(pl.multiple_of(b * 8, 8), 8)
            place8, held8 = rank[rows, :], wgt[rows, :]
            hit = [line == place8[j : j + 1, :] for j in range(4)]
            onehot = jnp.concatenate([jnp.where(m, 1.0, 0.0) for m in hit], axis=0)
            weight = jnp.concatenate(
                [jnp.where(hit[j], held8[j : j + 1, :], 0.0) for j in range(4)], axis=0
            )
            high = weight.astype(jnp.bfloat16)
            sel[b, 0 : 4 * CAP, :] = high
            sel[b, 4 * CAP :, :] = (weight - high.astype(jnp.float32)).astype(jnp.bfloat16)
            got = jnp.dot(
                onehot.astype(jnp.bfloat16), gv[b, 0:TOK, :], preferred_element_type=jnp.float32
            ).astype(jnp.bfloat16)
            at = pl.ds(pl.multiple_of(b * CAP, CAP), CAP)
            for j in range(4):
                xs[j, at, :] = got[j * CAP : (j + 1) * CAP, :]
            return 0

        lax.fori_loop(0, STEP, pick, 0, unroll=4)
    for j in range(4):
        pltpu.make_async_copy(wi.at[j], wiv.at[j], wsem.at[j]).wait()
        pltpu.make_async_copy(wo.at[j], wov.at[j], wsem.at[4 + j]).wait()

    def mlp(i, _):
        j, at = i // 2, pl.ds(pl.multiple_of(lax.rem(i, 2) * 256, 256), 256)
        both = jnp.dot(xs[j, at, :], wiv[j], preferred_element_type=jnp.float32)
        hidden = (jax.nn.silu(both[:, :H]) * both[:, H:]).astype(jnp.bfloat16)
        ys[j, at, :] = jnp.dot(hidden, wov[j], preferred_element_type=jnp.float32).astype(jnp.bfloat16)
        return 0

    lax.fori_loop(0, 8, mlp, 0, unroll=2)
    for n in range(nchunk):

        def spread(i, _):
            b = n * STEP + i
            at = pl.ds(pl.multiple_of(b * CAP, CAP), CAP)
            rows = jnp.concatenate([ys[j, at, :] for j in range(4)] * 2, axis=0)
            outv[b] = lax.dot_general(
                sel[b], rows, (((0,), (0,)), ((), ())), preferred_element_type=jnp.float32
            ).astype(jnp.bfloat16)
            return 0

        lax.fori_loop(0, STEP, spread, 0, unroll=4)
        pltpu.make_async_copy(outv.at[pl.ds(n * STEP, STEP)], part.at[pl.ds(n * STEP, STEP)], osem.at[n]).start()
    for n in range(nchunk):
        pltpu.make_async_copy(
            outv.at[pl.ds(n * STEP, STEP)], part.at[pl.ds(n * STEP, STEP)], osem.at[n]
        ).wait()


def experts_of(es, g, wi, wo):
    any_space = pl.BlockSpec(memory_space=pl.ANY)
    nchunk = CHIPS // STEP
    return pl.pallas_call(
        expert_kernel,
        out_shape=jax.ShapeDtypeStruct((CHIPS, TOK, D), jnp.bfloat16),
        in_specs=[pl.BlockSpec(memory_space=pltpu.SMEM)] + [any_space] * 3,
        out_specs=any_space,
        scratch_shapes=[
            pltpu.VMEM((CHIPS, ROWS, D), jnp.bfloat16),
            pltpu.VMEM((4, D, 2 * H), jnp.bfloat16),
            pltpu.VMEM((4, H, D), jnp.bfloat16),
            pltpu.VMEM((4, CHIPS * CAP, D), jnp.bfloat16),
            pltpu.VMEM((4, CHIPS * CAP, D), jnp.bfloat16),
            pltpu.VMEM((CHIPS * 8, TOK), jnp.float32),
            pltpu.VMEM((CHIPS * 8, TOK), jnp.float32),
            pltpu.VMEM((CHIPS * 8, TOK), jnp.float32),
            pltpu.VMEM((CHIPS, 8 * CAP, TOK), jnp.bfloat16),
            pltpu.VMEM((CHIPS, TOK, D), jnp.bfloat16),
            pltpu.SemaphoreType.DMA((nchunk,)),
            pltpu.SemaphoreType.DMA((8,)),
            pltpu.SemaphoreType.DMA((nchunk,)),
        ],
        compiler_params=pltpu.CompilerParams(vmem_limit_bytes=VMEM_LIMIT),
        cost_estimate=pl.CostEstimate(flops=6_000_000_000, bytes_accessed=40_000_000, transcendentals=0),
        name="experts",
    )(es, g, wi, wo)


def tiles_of(array):
    slots, columns = array.shape[0], array.shape[-1]
    rows = array.size // slots // columns
    tiled = array.reshape(slots, rows // 8, 8, columns // 128, 128)
    return tiled.transpose(0, 1, 3, 2, 4).reshape(slots, -1, 8, 128)


def untile(tiles, shape):
    slots, columns = shape[0], shape[-1]
    tiled = tiles.reshape(slots, -1, columns // 128, 8, 128)
    return tiled.transpose(0, 1, 3, 2, 4).reshape(shape)


def on_device(
    tokens, w_in, w_out, moments_in, moments_out, expert_ids, route_weights, old_plan, new_plan
):
    devices = lax.axis_size("exp")
    slots = 2 * devices
    slot_index = jnp.arange(slots, dtype=jnp.int32)
    same_expert = new_plan[:, None] == old_plan[None, :]
    source = jnp.min(jnp.where(same_expert, slot_index[None, :], slots), axis=1)

    state = [w_in, w_out, moments_in, moments_out]
    pooled = jnp.concatenate(
        [tiles_of(a) for a in state]
        + [jnp.zeros((2, CHIPS * CHUNK - TILES, 8, 128), jnp.bfloat16)],
        axis=1,
    )
    pooled = pooled.reshape(2, CHIPS, PIECE, 128).transpose(1, 0, 2, 3)

    share = route_weights / jnp.sum(route_weights, axis=1, keepdims=True)
    meta = jnp.concatenate(
        [
            expert_ids.T.astype(jnp.bfloat16),
            share.T.astype(jnp.bfloat16),
            (share.T - lax.reduce_precision(share.T, 8, 7)).astype(jnp.bfloat16),
            jnp.zeros((META, D - 3 * TOK), jnp.bfloat16),
        ],
        axis=1,
    )
    earlier = (old_plan[:, None] == old_plan[None, :]) & (slot_index[None, :] < slot_index[:, None])
    computes = jnp.where(jnp.any(earlier, axis=1), -1, old_plan)
    es = lax.dynamic_slice(computes, (lax.axis_index("exp") // 2 * 4,), (4,))
    sent = jnp.concatenate([tokens, meta], axis=0)
    g, gi, go, store = gather(sent, w_in, w_out, pooled)
    core = lax.axis_index("exp") % 2
    row = (source // 2 % 2 != core) * (2 * CHIPS) + source // 4 * 2 + source % 2
    picked = jnp.take(store.reshape(8 * CHIPS, PIECE // 2, 128), 2 * row + core, axis=0, mode="clip")
    picked, g = lax.optimization_barrier((picked, g))
    landed = lax.all_to_all(
        picked.reshape(devices, 2, PIECE // 2, 128), "exp", split_axis=0, concat_axis=0, tiled=True
    )
    mixed = reduce(experts_of(es, g, gi, go))
    tiles = landed.transpose(1, 0, 2, 3)
    tiles = tiles.reshape(2, CHIPS * CHUNK, 8, 128)
    outs, at = [], 0
    for a in state:
        count = a.size // 2 // 1024
        outs.append(untile(tiles[:, at : at + count], a.shape))
        at += count
    return (mixed, *outs)


def solution(mesh):
    return jax.shard_map(
        on_device,
        mesh=mesh,
        in_specs=(
            P(("grp", "exp"), None),
            P("exp", "grp", None),
            P("exp", "grp", None),
            P("exp", None, "grp", None),
            P("exp", None, "grp", None),
            P(("grp", "exp"), None),
            P(("grp", "exp"), None),
            P(),
            P(),
        ),
        out_specs=(
            P(("grp", "exp"), None),
            P("exp", "grp", None),
            P("exp", "grp", None),
            P("exp", None, "grp", None),
            P("exp", None, "grp", None),
        ),
        check_vma=False,
    )
```
